32 devices in a mesh: dp: 4 (over z), node: 2 (over y), chip: 4 (over x, core).
Axes of the slice: x: 2, y: 2, z: 4, core: 2. Of those that a mesh axis runs over, the one named last changes fastest.
Arguments:
- se_gate: bfloat16 [4096, 2048], P(('dp', 'node', 'chip')), parts along dimension 0, may hold values from -6 to 6
- se_key: bfloat16 [4096, 2048], P(('dp', 'node', 'chip')), parts along dimension 0, may hold values from -6 to 6
- se_value: bfloat16 [4096, 2048], P(('dp', 'node', 'chip')), parts along dimension 0, may hold values from -6 to 6
- li_gate: bfloat16 [4096, 2048], P(('dp', 'node', 'chip')), parts along dimension 0, may hold values from -6 to 6
- li_key: bfloat16 [4096, 2048], P(('dp', 'node', 'chip')), parts along dimension 0, may hold values from -6 to 6
- li_value: bfloat16 [4096, 2048], P(('dp', 'node', 'chip')), parts along dimension 0, may hold values from -6 to 6
- se_feature: float32 [3, 3, 2048], replicated, may hold values from -3 to 3
- se_filter: float32 [7, 2048], replicated, may hold values from -2 to 2
- li_feature: float32 [3, 3, 2048], replicated, may hold values from -3 to 3
- li_residue: float32 [16, 2048], replicated, may hold values from -1.25 to 1.25
- li_rate: float32 [16, 2048], replicated, may hold values from 4.8828125e-05 to 0.08, as said below
- li_skip: float32 [2048], replicated, may hold values from -4 to 4
Outputs:
- se_out: bfloat16 [4096, 2048], P(('dp', 'node', 'chip')), parts along dimension 0
- li_out: bfloat16 [4096, 2048], P(('dp', 'node', 'chip')), parts along dimension 0
The draws below stay inside these ranges and needn't reach their ends.
There are 4 independent parts, one for each index of `dp`. The reference program is written for one: setup_inputs(seed, part) draws one part's arguments, and reference() takes and returns one part's arrays. A program takes and returns all parts, laid end to end along the dimension named above; an argument that names none is the same for every part. Nothing has to cross between parts.
Inputs may be any that keep to these rules, and one draw needn't show every extreme that they name: `li_rate`: positive decay rates.
All inputs are finite; a program needn't handle non-finite values.
Results may differ from the reference program's by a relative error of at most 0.0055.
Values may be sent and summed in bfloat16 or wider, within the bound.
A program may use at most 128 MiB of HBM per device.

```python
import math
import jax
import jax.numpy as jnp
from jax import lax

CH = 2048
M = 16
SE_TAPS = 7
FEAT_TAPS = 3
LENGTH = 1024


def draw_li_rate(key, part):
    first, second, third = jax.random.split(jax.random.fold_in(key, 11), 3)
    slow = jnp.exp(jax.random.uniform(first, (M, CH), jnp.float32, math.log(0.05 / LENGTH), math.log(1.5 / LENGTH)))
    quick = jnp.exp(jax.random.uniform(second, (M, CH), jnp.float32, math.log(0.02), math.log(0.08)))
    share = 0.5
    picked = jax.random.uniform(third, (M, CH), jnp.float32) < share
    return jnp.where(picked, slow, quick).astype(jnp.float32)


def levels(key, dims, cuts, least, largest):
    def one(dim, parts):
        heights = jax.random.uniform(jax.random.fold_in(jax.random.fold_in(key, 6), dim), (parts,), jnp.float32, least / len(cuts), largest / len(cuts))
        return jnp.repeat(jnp.exp(heights), dims[dim] // parts).reshape((-1,) + (1,) * (len(dims) - dim - 1))

    gain = one(*cuts[0])
    for cut in cuts[1:]:
        gain = gain * one(*cut)
    return gain


def noise(key, shape, deviation, most, shards=(), held_as=jnp.bfloat16):
    entries = jax.random.normal(key, shape, jnp.float32) * deviation
    if len(shards) > 0:
        entries = levels(key, shape, shards, -0.22, 0.18) * entries
    return jnp.clip(entries, min=-most, max=most).astype(held_as)


def setup_inputs(seed: int = 0, part: int = 0) -> dict:
    arg_keys = jax.random.split(jax.random.key(seed), 13)
    part_splits = jax.random.split(jax.random.fold_in(arg_keys[12], part), 13)
    return {
        "se_gate": noise(part_splits[0], (LENGTH, CH), 1.0, 6.0, ((0, 8),)),
        "se_key": noise(part_splits[1], (LENGTH, CH), 1.0, 6.0, ((0, 8),)),
        "se_value": noise(part_splits[2], (LENGTH, CH), 1.0, 6.0, ((0, 8),)),
        "li_gate": noise(part_splits[3], (LENGTH, CH), 1.0, 6.0, ((0, 8),)),
        "li_key": noise(part_splits[4], (LENGTH, CH), 1.0, 6.0, ((0, 8),)),
        "li_value": noise(part_splits[5], (LENGTH, CH), 1.0, 6.0, ((0, 8),)),
        "se_feature": noise(arg_keys[6], (FEAT_TAPS, 3, CH), 0.6, 3.0, (), jnp.float32),
        "se_filter": noise(arg_keys[7], (SE_TAPS, CH), 0.4, 2.0, (), jnp.float32),
        "li_feature": noise(arg_keys[8], (FEAT_TAPS, 3, CH), 0.6, 3.0, (), jnp.float32),
        "li_residue": noise(arg_keys[9], (M, CH), 0.25, 1.25, (), jnp.float32),
        "li_rate": draw_li_rate(jax.random.fold_in(arg_keys[12], 71), part),
        "li_skip": noise(arg_keys[11], (CH,), 1.0, 4.0, (), jnp.float32),
    }


def delayed(field, lag):
    if lag == 0:
        return field
    empty = jnp.zeros((lag,) + field.shape[1:], field.dtype)
    return jnp.concatenate([empty, field[:-lag]], axis=0)

def causal_taps(field, taps):
    total = taps[0] * field
    for lag in range(1, taps.shape[0]):
        total = total + taps[lag] * delayed(field, lag)
    return total

def implicit_conv(values, residue, rate):
    length = values.shape[0]
    groups = values.shape[1] // 128
    modes = residue.shape[0]
    vblocks = values.reshape(length, groups, 128).transpose(1, 0, 2)
    rblocks = residue.reshape(modes, groups, 128).transpose(1, 0, 2)
    ablocks = rate.reshape(modes, groups, 128).transpose(1, 0, 2)

    def one_group(args):
        piece, resid, decay = args
        steps = jnp.arange(length, dtype=jnp.float32)
        weight = resid * jnp.sqrt(-jnp.expm1(-2.0 * decay))
        filt = lax.optimization_barrier(jnp.sum(weight[None] * jnp.exp(-steps[:, None, None] * decay[None]), axis=1))
        total = 2 * length
        spectrum = jnp.fft.rfft(piece, total, axis=0) * jnp.fft.rfft(filt, total, axis=0)
        return jnp.fft.irfft(spectrum, total, axis=0)[:length]
    result = lax.map(one_group, (vblocks, rblocks, ablocks))
    return result.transpose(1, 0, 2).reshape(length, groups * 128)

def reference(se_gate, se_key, se_value, li_gate, li_key, li_value, se_feature, se_filter, li_feature, li_residue, li_rate, li_skip):
    se_g = causal_taps(se_gate.astype(jnp.float32), se_feature[:, 0])
    se_k = causal_taps(se_key.astype(jnp.float32), se_feature[:, 1])
    se_v = causal_taps(se_value.astype(jnp.float32), se_feature[:, 2])
    u_se = (se_k * se_v).astype(jnp.bfloat16)
    mixed = causal_taps(u_se.astype(jnp.float32), se_filter)
    se_out = (se_g * mixed).astype(jnp.bfloat16)
    li_g = causal_taps(li_gate.astype(jnp.float32), li_feature[:, 0])
    li_k = causal_taps(li_key.astype(jnp.float32), li_feature[:, 1])
    li_v = causal_taps(li_value.astype(jnp.float32), li_feature[:, 2])
    u_li = (li_k * li_v).astype(jnp.bfloat16)
    flat = u_li.astype(jnp.float32)
    conv = implicit_conv(flat, li_residue, li_rate)
    li_out = (li_g * (conv + li_skip * flat)).astype(jnp.bfloat16)
    return (se_out, li_out)
```

```python
import functools

import jax
import jax.numpy as jnp
from jax import lax
from jax.experimental import pallas as pl
from jax.experimental.pallas import tpu as pltpu
from jax.sharding import PartitionSpec as P

LANES = 128
SUB = 8
LINK = jnp.bfloat16
GROUP = ("node", "chip")


def mixer(n, chips, *refs):
    streams, kept = refs[:6], refs[6:12]
    se, partial, gates, terms, starts, shift, carry, hops = refs[12:20]
    (
        held, halo, arrived, sent, ext, extended, u_li, near, carried, own, inner,
        se_feature, se_filter, li_feature, residue, rate, skip, in_sem, part_sem, fixed_sem, halo_send, halo_recv, pair_send, pair_recv, state_send, state_recv,
    ) = refs[20:]
    rows, width = held.shape[1], held.shape[2]
    blocks = width // LANES
    chunks = rows // SUB
    modes = rate.shape[0]
    lags = se_filter.shape[0]
    pair = 2 if n % 2 == 0 else 1
    dp = lax.axis_index("dp")
    me = lax.axis_index("node") * chips + lax.axis_index("chip")

    def device(index):
        return (dp, lax.div(index, chips), lax.rem(index, chips))

    order = (4, 5, 1, 2, 0, 3)
    parts = part_sem.shape[1]
    each = width // parts
    loads = [pltpu.make_async_copy(streams[i], held.at[i], in_sem.at[i]) for i in range(4)]

    def piece(i, part):
        cols = pl.ds(part * each, each)
        return pltpu.make_async_copy(streams[i].at[:, cols], held.at[i, :, cols], part_sem.at[i - 4, part])

    fixed = (se_feature, se_filter, li_feature, residue, rate, skip)
    fixed_loads = [pltpu.make_async_copy(kept[i], fixed[i], fixed_sem.at[i]) for i in range(6)]
    for i in (4, 2):
        fixed_loads[i].start()
    for part in range(parts):
        for i in (4, 5):
            piece(i, part).start()

    barrier = pltpu.get_barrier_semaphore()

    @pl.loop(0, n)
    def _(other):
        @pl.when(other != me)
        def _():
            pl.semaphore_signal(barrier, inc=1, device_id=device(other), device_id_type=pl.DeviceIdType.MESH)

    for i in range(6):
        ext[i, pl.ds(0, 2 * SUB)] = jnp.zeros((2 * SUB, LANES), jnp.float32)

    def columns(c):
        return pl.ds(pl.multiple_of(c * LANES, LANES), LANES)

    def featurized(i, c, taps, stream, early):
        cols = columns(c)
        if i not in (4, 5):
            ext[i, pl.ds(SUB, SUB)] = halo[i, :, cols].astype(jnp.float32)
        ext[i, pl.ds(2 * SUB, rows)] = held[i, :, cols].astype(jnp.float32)
        first, count = 2 * SUB - early, rows + early
        total = taps[0, pl.ds(stream, 1), cols] * ext[i, pl.ds(first, count)]
        for lag in (1, 2):
            total = total + taps[lag, pl.ds(stream, 1), cols] * ext[i, pl.ds(first - lag, count)]
        return total

    def local_states(c):
        cols = columns(c)
        product = featurized(4, c, li_feature, 1, 0) * featurized(5, c, li_feature, 2, 0)
        u_li[c, pl.ds(0, SUB)] = jnp.zeros((SUB, LANES), jnp.float32)
        u_li[c, pl.ds(SUB, rows)] = product.astype(jnp.bfloat16).astype(jnp.float32)
        pace = rate[:, cols]
        powers = [None] + [jnp.exp(-pace * float(k)) for k in range(1, SUB + 1)]
        state = jnp.zeros((modes, LANES), jnp.float32)
        for a in range(chunks):
            starts[c, a] = state
            new = jnp.broadcast_to(u_li[c, pl.ds(SUB + a * SUB + SUB - 1, 1)], (modes, LANES))
            for b in range(SUB - 1):
                new = new + powers[SUB - 1 - b] * u_li[c, pl.ds(SUB + a * SUB + b, 1)]
            state = powers[SUB] * state + new
        own[c] = state

    def stage(part):
        for i in (4, 5):
            piece(i, part).wait()

        @pl.loop(part * (blocks // parts), (part + 1) * (blocks // parts))
        def _(c):
            local_states(c)

    for i in (4, 2):
        fixed_loads[i].wait()
    for i in (3, 5, 0, 1):
        fixed_loads[i].start()
    stage(0)
    for i in (1, 2, 0, 3):
        loads[i].start()
    pl.semaphore_wait(barrier, n - 1)

    def halo_copy(i):
        return pltpu.make_async_remote_copy(
            src_ref=streams[i].at[pl.ds(rows - SUB, SUB)],
            dst_ref=halo.at[i],
            send_sem=halo_send.at[i],
            recv_sem=halo_recv.at[i],
            device_id=device(lax.rem(me + 1, n)),
            device_id_type=pl.DeviceIdType.MESH,
        )

    @pl.when(me < n - 1)
    def _():
        for i in order:
            halo_copy(i).start()

    @pl.when(me == 0)
    def _():
        halo[...] = jnp.zeros_like(halo)

    if pair == 2:
        @pl.when(lax.rem(me, 2) == 0)
        def _():
            inner[...] = jnp.zeros_like(inner)


    place = lax.broadcasted_iota(jnp.int32, (SUB, LANES), 0)
    step = place.astype(jnp.float32)

    def ready(i):
        @pl.when(me > 0)
        def _():
            halo_copy(i).wait_recv()

    for part in range(1, parts):
        stage(part)

    ready(4)
    ready(5)

    wide = 4 if blocks % 4 == 0 else 1

    def fixed_up(c, j):
        cols = columns(c)

        def opening(i, stream):
            at = 2 * j + i - 4
            ext[at, pl.ds(SUB, SUB)] = halo[i, :, cols].astype(jnp.float32)
            ext[at, pl.ds(2 * SUB, SUB)] = held[i, pl.ds(0, SUB), cols].astype(jnp.float32)
            total = li_feature[0, pl.ds(stream, 1), cols] * ext[at, pl.ds(2 * SUB, SUB)]
            for lag in (1, 2):
                total = total + li_feature[lag, pl.ds(stream, 1), cols] * ext[at, pl.ds(2 * SUB - lag, SUB)]
            return total

        right = (opening(4, 1) * opening(5, 2)).astype(jnp.bfloat16).astype(jnp.float32)
        extended[pl.ds(j * SUB, SUB)] = right - u_li[c, pl.ds(SUB, SUB)]
        u_li[c, pl.ds(SUB, SUB)] = right
        pace = rate[:, cols]
        moved = jnp.exp(-pace * float(SUB - 1)) * extended[pl.ds(j * SUB, 1)]
        moved = moved + jnp.exp(-pace * float(SUB - 2)) * extended[pl.ds(j * SUB + 1, 1)]
        shift[c] = moved
        state = own[c] + jnp.exp(-pace * float(rows - SUB)) * moved
        own[c] = state
        sent[c] = state.astype(sent.dtype)

    @pl.loop(0, blocks // wide)
    def _(many):
        for j in range(wide):
            fixed_up(many * wide + j, j)

    def state_copy(source, target):
        return pltpu.make_async_remote_copy(
            src_ref=sent,
            dst_ref=arrived.at[source],
            send_sem=state_send.at[target],
            recv_sem=state_recv.at[source],
            device_id=device(target),
            device_id_type=pl.DeviceIdType.MESH,
        )

    def pair_copy():
        return pltpu.make_async_remote_copy(
            src_ref=sent,
            dst_ref=inner,
            send_sem=pair_send.at[0],
            recv_sem=pair_recv.at[0],
            device_id=device(me + 1 - 2 * lax.rem(me, 2)),
            device_id_type=pl.DeviceIdType.MESH,
        )

    if pair == 2:
        @pl.when(lax.rem(me, 2) == 0)
        def _():
            pair_copy().start()

    for i in (3, 5, 0, 1):
        fixed_loads[i].wait()

    @pl.loop(0, blocks)
    def _(c):
        cols = columns(c)
        pace = rate[:, cols]
        twice = 2.0 * pace
        small = twice * (1.0 - twice * (0.5 - twice * (1.0 / 6.0 - twice * (1.0 / 24.0 - twice * (1.0 / 120.0)))))
        gap = jnp.where(twice < 0.03125, small, 1.0 - jnp.exp(-twice))
        carried[c] = residue[:, cols] * jnp.sqrt(gap)
        total = jnp.zeros((SUB, LANES), jnp.float32)
        for m in range(modes):
            speed = rate[pl.ds(m, 1), cols]
            term = carried[c, pl.ds(m, 1)] * jnp.exp(-speed * step)
            total = total + term
            terms[c, m] = term * jnp.exp(-speed)
        near[c, 0] = total
        for lag in range(SUB - 1, -1, -1):
            tap = near[c, 0, pl.ds(lag, 1)]
            if lag == 0:
                tap = tap + skip[:, cols]
            near[c, lag] = jnp.where(place >= lag, jnp.broadcast_to(tap, (SUB, LANES)), 0.0)

    if pair == 2:
        @pl.when(lax.rem(me, 2) == 1)
        def _():
            pair_copy().wait_recv()

            @pl.loop(0, blocks)
            def _(c):
                fall = jnp.exp(-rate[:, columns(c)] * float(rows))
                sent[c] = (fall * inner[c].astype(jnp.float32) + own[c]).astype(sent.dtype)

    leads = lax.rem(me, pair) == pair - 1
    slot = lax.div(me, pair)

    @pl.when(leads)
    def _():
        @pl.loop(me + 1, n)
        def _(target):
            state_copy(slot, n + me - target).start()

    for i in (1, 2, 0, 3):
        loads[i].wait()
        ready(i)

    @pl.loop(0, blocks)
    def _(c):
        cols = columns(c)
        product = featurized(1, c, se_feature, 1, SUB) * featurized(2, c, se_feature, 2, SUB)
        extended[...] = product.astype(jnp.bfloat16).astype(jnp.float32)
        mixed = se_filter[pl.ds(0, 1), cols] * extended[pl.ds(SUB, rows)]
        for lag in range(1, lags):
            mixed = mixed + se_filter[pl.ds(lag, 1), cols] * extended[pl.ds(SUB - lag, rows)]
        se[:, cols] = (featurized(0, c, se_feature, 0, 0) * mixed).astype(jnp.bfloat16)
        gates[c] = featurized(3, c, li_feature, 0, 0)
        taps = [near[c, lag] for lag in range(SUB)]
        for a in range(chunks):
            total = taps[0] * u_li[c, pl.ds(SUB + a * SUB, SUB)]
            for lag in range(1, SUB):
                total = total + taps[lag] * u_li[c, pl.ds(SUB + a * SUB - lag, SUB)]
            partial[c, pl.ds(a * SUB, SUB)] = total

    odd = lax.rem(jnp.full((modes, LANES), me, jnp.int32), 2) == 1

    @pl.loop(0, slot)
    def _(source):
        state_copy(source, me).wait_recv()

    def carried_in(c):
        pace = rate[:, columns(c)]
        fall = jnp.exp(-pace * float(rows * pair))

        def add(source, total):
            return fall * total + arrived[source, c].astype(jnp.float32)

        earlier = lax.fori_loop(0, slot, add, jnp.zeros((modes, LANES), jnp.float32))
        if pair == 2:
            within = jnp.exp(-pace * float(rows)) * earlier + inner[c].astype(jnp.float32)
            earlier = jnp.where(odd, within, earlier)
        carry[c] = earlier
        hops[c] = jnp.exp(-pace * float(SUB))

    @pl.loop(0, blocks)
    def _(c):
        carried_in(c)

    @pl.when(me < n - 1)
    def _():
        for i in range(6):
            halo_copy(i).wait_send()

    if pair == 2:
        @pl.when(lax.rem(me, 2) == 0)
        def _():
            pair_copy().wait_send()

    @pl.when(leads)
    def _():
        @pl.loop(me + 1, n)
        def _(target):
            state_copy(slot, target).wait_send()


def finish(se, partial, gates, terms, starts, shift, carry, hops, se_out, li_out, made, full, sems):
    blocks, rows = partial.shape[0], partial.shape[1]
    chunks, modes = starts.shape[1], starts.shape[2]
    parts = sems.shape[0] - 1
    each = made.shape[1] // parts
    whole = pltpu.make_async_copy(se, se_out, sems.at[parts])
    whole.start()

    def far(c):
        earlier = carry[c]
        hop = hops[c]
        for a in range(chunks):
            full[a] = starts[c, a] + earlier
            earlier = hop * earlier
            if a == 0:
                earlier = earlier + shift[c]
        cols = pl.ds(pl.multiple_of(c * LANES, LANES), LANES)
        for top in range(0, chunks, SUB):
            span = range(top, min(top + SUB, chunks))
            totals = [partial[c, pl.ds(a * SUB, SUB)] for a in span]
            for m in range(modes):
                term = terms[c, m]
                totals = [total + term * full[a, pl.ds(m, 1)] for a, total in zip(span, totals)]
            first = pl.ds(top * SUB, len(span) * SUB)
            made[first, cols] = (gates[c, first] * jnp.concatenate(totals)).astype(jnp.bfloat16)

    def piece(part):
        cols = pl.ds(part * each, each)
        return pltpu.make_async_copy(made.at[:, cols], li_out.at[:, cols], sems.at[part])

    for part in range(parts):
        @pl.loop(part * (blocks // parts), (part + 1) * (blocks // parts))
        def _(c):
            far(c)

        piece(part).start()
    for part in range(parts):
        piece(part).wait()
    whole.wait()


def shards(*args):
    rows, width = args[0].shape
    modes = args[10].shape[0]
    n, chips = lax.axis_size(GROUP), lax.axis_size("chip")
    blocks, chunks = width // LANES, rows // SUB
    f32 = jnp.float32
    far = pl.BlockSpec(memory_space=pltpu.HBM)
    local = pl.BlockSpec(memory_space=pltpu.VMEM)
    operands = args[:11] + (args[11][None],)
    words = rows * width * 10 + width * modes * (3 * chunks + 3 * SUB + 8 + n)
    budget = min(4 * words + 8 * 2**20, 60 * 2**20)
    parts = 4 if blocks % 4 == 0 else 1
    passed = ((rows, width), jnp.bfloat16), *(((blocks, *shape, LANES), f32) for shape in ((rows,), (rows,), (modes, SUB), (chunks, modes), (modes,), (modes,), (modes,)))
    mixed = pl.pallas_call(
        functools.partial(mixer, n, chips),
        out_shape=tuple(jax.ShapeDtypeStruct(*one) for one in passed),
        in_specs=[far] * 12,
        out_specs=(local,) * len(passed),
        scratch_shapes=[
            pltpu.VMEM((6, rows, width), jnp.bfloat16),
            pltpu.VMEM((6, SUB, width), jnp.bfloat16),
            pltpu.VMEM((n, blocks, modes, LANES), LINK),
            pltpu.VMEM((blocks, modes, LANES), LINK),
            pltpu.VMEM((8, rows + 2 * SUB, LANES), f32),
            pltpu.VMEM((rows + SUB, LANES), f32),
            pltpu.VMEM((blocks, rows + SUB, LANES), f32),
            pltpu.VMEM((blocks, SUB, SUB, LANES), f32),
            pltpu.VMEM((blocks, modes, LANES), f32),
            pltpu.VMEM((blocks, modes, LANES), f32),
            pltpu.VMEM((blocks, modes, LANES), LINK),
            *[pltpu.VMEM(array.shape, f32) for array in operands[6:]],
            pltpu.SemaphoreType.DMA((4,)),
            pltpu.SemaphoreType.DMA((2, parts)),
            pltpu.SemaphoreType.DMA((6,)),
            pltpu.SemaphoreType.DMA((6,)),
            pltpu.SemaphoreType.DMA((6,)),
            pltpu.SemaphoreType.DMA((1,)),
            pltpu.SemaphoreType.DMA((1,)),
            pltpu.SemaphoreType.DMA((n,)),
            pltpu.SemaphoreType.DMA((n,)),
        ],
        compiler_params=pltpu.CompilerParams(collective_id=0, has_side_effects=True, vmem_limit_bytes=budget),
        name="mixer",
    )(*(pltpu.with_memory_space_constraint(array, pltpu.HBM) for array in operands))
    return pl.pallas_call(
        finish,
        out_shape=(jax.ShapeDtypeStruct((rows, width), jnp.bfloat16),) * 2,
        in_specs=[local] * len(passed),
        out_specs=(far, far),
        scratch_shapes=[
            pltpu.VMEM((rows, width), jnp.bfloat16),
            pltpu.VMEM((chunks, modes, LANES), f32),
            pltpu.SemaphoreType.DMA((parts + 1,)),
        ],
        compiler_params=pltpu.CompilerParams(vmem_limit_bytes=8 * 2**20),
        name="finish",
    )(*mixed)


def solution(mesh):
    placed = (P(("dp", "node", "chip"), None),) * 6 + (P(),) * 6
    return jax.shard_map(
        shards,
        mesh=mesh,
        in_specs=placed,
        out_specs=(P(("dp", "node", "chip"), None), P(("dp", "node", "chip"), None)),
        check_vma=False,
    )
```

```python
import functools

import jax
import jax.numpy as jnp
from jax import lax
from jax.experimental import pallas as pl
from jax.experimental.pallas import tpu as pltpu
from jax.sharding import PartitionSpec as P

LANES = 128
SUB = 8
LINK = jnp.bfloat16
GROUP = ("node", "chip")


def mixer(n, chips, *refs):
    streams, kept = refs[:6], refs[6:12]
    se, partial, gates, terms, starts, shift, carry, hops = refs[12:20]
    (
        held, halo, arrived, sent, ext, extended, u_li, near, carried, own, inner,
        se_feature, se_filter, li_feature, residue, rate, skip, in_sem, part_sem, fixed_sem, halo_send, halo_recv, pair_send, pair_recv, state_send, state_recv, ready_sem,
    ) = refs[20:]
    rows, width = held.shape[1], held.shape[2]
    blocks = width // LANES
    chunks = rows // SUB
    modes = rate.shape[0]
    lags = se_filter.shape[0]
    pair = 2 if n % 2 == 0 else 1
    dp = lax.axis_index("dp")
    me = lax.axis_index("node") * chips + lax.axis_index("chip")

    def device(index):
        return (dp, lax.div(index, chips), lax.rem(index, chips))

    order = (4, 5, 1, 2, 0, 3)
    parts = part_sem.shape[1]
    each = width // parts
    loads = [pltpu.make_async_copy(streams[i], held.at[i], in_sem.at[i]) for i in range(4)]

    def piece(i, part):
        cols = pl.ds(part * each, each)
        return pltpu.make_async_copy(streams[i].at[:, cols], held.at[i, :, cols], part_sem.at[i - 4, part])

    fixed = (se_feature, se_filter, li_feature, residue, rate, skip)
    fixed_loads = [pltpu.make_async_copy(kept[i], fixed[i], fixed_sem.at[i]) for i in range(6)]
    for i in (4, 2):
        fixed_loads[i].start()
    for part in range(parts):
        for i in (4, 5):
            piece(i, part).start()

    barrier = pltpu.get_barrier_semaphore()

    odd_core = lax.rem(me, 2) == 1

    def hail(semaphore, other):
        pl.semaphore_signal(semaphore, inc=1, device_id=device(other), device_id_type=pl.DeviceIdType.MESH)

    def hail_if(condition, semaphore, other):
        @pl.when(condition)
        def _():
            hail(semaphore, other)

    if pair == 2:
        hail_if(me > 0, barrier, me - 1)
        hail_if(odd_core & (me > 1), barrier, me - 2)
        hail_if(odd_core & (me < n - 1), barrier, me + 2)
    else:
        @pl.loop(0, n)
        def _(other):
            hail_if(other != me, barrier, other)

    def meet():
        if pair == 2:
            pl.semaphore_wait(barrier, jnp.where(odd_core, 2 * (me < n - 1).astype(jnp.int32) + (me > 1).astype(jnp.int32), 1))
            if n > 4:
                hail_if(me == n - 3, ready_sem, me - 2)
        else:
            pl.semaphore_wait(barrier, n - 1)

    for i in range(6):
        ext[i, pl.ds(0, 2 * SUB)] = jnp.zeros((2 * SUB, LANES), jnp.float32)

    def columns(c):
        return pl.ds(pl.multiple_of(c * LANES, LANES), LANES)

    def featurized(i, c, taps, stream, early):
        cols = columns(c)
        if i not in (4, 5):
            ext[i, pl.ds(SUB, SUB)] = halo[i, :, cols].astype(jnp.float32)
        ext[i, pl.ds(2 * SUB, rows)] = held[i, :, cols].astype(jnp.float32)
        first, count = 2 * SUB - early, rows + early
        total = taps[0, pl.ds(stream, 1), cols] * ext[i, pl.ds(first, count)]
        for lag in (1, 2):
            total = total + taps[lag, pl.ds(stream, 1), cols] * ext[i, pl.ds(first - lag, count)]
        return total

    def local_states(c):
        cols = columns(c)
        product = featurized(4, c, li_feature, 1, 0) * featurized(5, c, li_feature, 2, 0)
        u_li[c, pl.ds(0, SUB)] = jnp.zeros((SUB, LANES), jnp.float32)
        u_li[c, pl.ds(SUB, rows)] = product.astype(jnp.bfloat16).astype(jnp.float32)
        pace = rate[:, cols]
        powers = [None] + [jnp.exp(-pace * float(k)) for k in range(1, SUB + 1)]
        state = jnp.zeros((modes, LANES), jnp.float32)
        for a in range(chunks):
            starts[c, a] = state
            new = jnp.broadcast_to(u_li[c, pl.ds(SUB + a * SUB + SUB - 1, 1)], (modes, LANES))
            for b in range(SUB - 1):
                new = new + powers[SUB - 1 - b] * u_li[c, pl.ds(SUB + a * SUB + b, 1)]
            state = powers[SUB] * state + new
        own[c] = state

    def halo_copy(i):
        return pltpu.make_async_remote_copy(
            src_ref=streams[i].at[pl.ds(rows - SUB, SUB)],
            dst_ref=halo.at[i],
            send_sem=halo_send.at[i],
            recv_sem=halo_recv.at[i],
            device_id=device(lax.rem(me + 1, n)),
            device_id_type=pl.DeviceIdType.MESH,
        )

    per = blocks // parts

    def states(first, last):
        @pl.loop(first, last)
        def _(c):
            local_states(c)

    for i in (4, 2):
        fixed_loads[i].wait()
    for part in range(parts):
        for i in (4, 5):
            piece(i, part).wait()
        if part == 0:
            for i in (3, 5, 0, 1):
                fixed_loads[i].start()
            for i in (1, 2, 0, 3):
                loads[i].start()
            states(0, per // 2)
            meet()

            @pl.when(me < n - 1)
            def _():
                for i in order:
                    halo_copy(i).start()

            states(per // 2, per)
        else:
            states(part * per, (part + 1) * per)

    if pair == 2:
        @pl.when(odd_core & (me > 1) & (me < n - 4))
        def _():
            pl.semaphore_wait(ready_sem, 1)
            hail(ready_sem, me - 2)

    @pl.when(me == 0)
    def _():
        halo[...] = jnp.zeros_like(halo)

    if pair == 2:
        @pl.when(lax.rem(me, 2) == 0)
        def _():
            inner[...] = jnp.zeros_like(inner)


    place = lax.broadcasted_iota(jnp.int32, (SUB, LANES), 0)
    step = place.astype(jnp.float32)

    def ready(i):
        @pl.when(me > 0)
        def _():
            halo_copy(i).wait_recv()

    ready(4)
    ready(5)

    wide = 4 if blocks % 4 == 0 else 1

    def fixed_up(c, j):
        cols = columns(c)

        def opening(i, stream):
            at = 2 * j + i - 4
            ext[at, pl.ds(SUB, SUB)] = halo[i, :, cols].astype(jnp.float32)
            ext[at, pl.ds(2 * SUB, SUB)] = held[i, pl.ds(0, SUB), cols].astype(jnp.float32)
            total = li_feature[0, pl.ds(stream, 1), cols] * ext[at, pl.ds(2 * SUB, SUB)]
            for lag in (1, 2):
                total = total + li_feature[lag, pl.ds(stream, 1), cols] * ext[at, pl.ds(2 * SUB - lag, SUB)]
            return total

        right = (opening(4, 1) * opening(5, 2)).astype(jnp.bfloat16).astype(jnp.float32)
        extended[pl.ds(j * SUB, SUB)] = right - u_li[c, pl.ds(SUB, SUB)]
        u_li[c, pl.ds(SUB, SUB)] = right
        pace = rate[:, cols]
        moved = jnp.exp(-pace * float(SUB - 1)) * extended[pl.ds(j * SUB, 1)]
        moved = moved + jnp.exp(-pace * float(SUB - 2)) * extended[pl.ds(j * SUB + 1, 1)]
        shift[c] = moved
        state = own[c] + jnp.exp(-pace * float(rows - SUB)) * moved
        own[c] = state
        sent[c] = state.astype(sent.dtype)

    @pl.loop(0, blocks // wide)
    def _(many):
        for j in range(wide):
            fixed_up(many * wide + j, j)

    def state_copy(source, target):
        return pltpu.make_async_remote_copy(
            src_ref=sent,
            dst_ref=arrived.at[source],
            send_sem=state_send.at[target],
            recv_sem=state_recv.at[source],
            device_id=device(target),
            device_id_type=pl.DeviceIdType.MESH,
        )

    def pair_copy():
        return pltpu.make_async_remote_copy(
            src_ref=sent,
            dst_ref=inner,
            send_sem=pair_send.at[0],
            recv_sem=pair_recv.at[0],
            device_id=device(me + 1 - 2 * lax.rem(me, 2)),
            device_id_type=pl.DeviceIdType.MESH,
        )

    if pair == 2:
        @pl.when(lax.rem(me, 2) == 0)
        def _():
            pair_copy().start()

    for i in (3, 5, 0, 1):
        fixed_loads[i].wait()

    @pl.loop(0, blocks)
    def _(c):
        cols = columns(c)
        pace = rate[:, cols]
        twice = 2.0 * pace
        small = twice * (1.0 - twice * (0.5 - twice * (1.0 / 6.0 - twice * (1.0 / 24.0 - twice * (1.0 / 120.0)))))
        gap = jnp.where(twice < 0.03125, small, 1.0 - jnp.exp(-twice))
        carried[c] = residue[:, cols] * jnp.sqrt(gap)
        total = jnp.zeros((SUB, LANES), jnp.float32)
        for m in range(modes):
            speed = rate[pl.ds(m, 1), cols]
            term = carried[c, pl.ds(m, 1)] * jnp.exp(-speed * step)
            total = total + term
            terms[c, m] = term * jnp.exp(-speed)
        near[c, 0] = total
        for lag in range(SUB - 1, -1, -1):
            tap = near[c, 0, pl.ds(lag, 1)]
            if lag == 0:
                tap = tap + skip[:, cols]
            near[c, lag] = jnp.where(place >= lag, jnp.broadcast_to(tap, (SUB, LANES)), 0.0)

    if pair == 2:
        @pl.when(lax.rem(me, 2) == 1)
        def _():
            pair_copy().wait_recv()

            @pl.loop(0, blocks)
            def _(c):
                fall = jnp.exp(-rate[:, columns(c)] * float(rows))
                sent[c] = (fall * inner[c].astype(jnp.float32) + own[c]).astype(sent.dtype)

    leads = lax.rem(me, pair) == pair - 1
    slot = lax.div(me, pair)

    def send_states(first, last):
        @pl.when(leads)
        def _():
            @pl.loop(first, last)
            def _(target):
                state_copy(slot, target).start()

    if pair == 2:
        send_states(me + 1, jnp.minimum(me + 3, n))

        if n > 4:
            @pl.when(me == 1)
            def _():
                pl.semaphore_wait(ready_sem, 1)

        send_states(me + 3, n)
    else:
        send_states(me + 1, n)

    for i in (1, 2, 0, 3):
        loads[i].wait()
        ready(i)

    @pl.loop(0, blocks)
    def _(c):
        cols = columns(c)
        product = featurized(1, c, se_feature, 1, SUB) * featurized(2, c, se_feature, 2, SUB)
        extended[...] = product.astype(jnp.bfloat16).astype(jnp.float32)
        mixed = se_filter[pl.ds(0, 1), cols] * extended[pl.ds(SUB, rows)]
        for lag in range(1, lags):
            mixed = mixed + se_filter[pl.ds(lag, 1), cols] * extended[pl.ds(SUB - lag, rows)]
        se[:, cols] = (featurized(0, c, se_feature, 0, 0) * mixed).astype(jnp.bfloat16)
        gates[c] = featurized(3, c, li_feature, 0, 0)
        taps = [near[c, lag] for lag in range(SUB)]
        for a in range(chunks):
            total = taps[0] * u_li[c, pl.ds(SUB + a * SUB, SUB)]
            for lag in range(1, SUB):
                total = total + taps[lag] * u_li[c, pl.ds(SUB + a * SUB - lag, SUB)]
            partial[c, pl.ds(a * SUB, SUB)] = total

    odd = lax.rem(jnp.full((modes, LANES), me, jnp.int32), 2) == 1

    @pl.loop(0, slot)
    def _(source):
        state_copy(source, me).wait_recv()

    def carried_in(c):
        pace = rate[:, columns(c)]
        fall = jnp.exp(-pace * float(rows * pair))

        def add(source, total):
            return fall * total + arrived[source, c].astype(jnp.float32)

        earlier = lax.fori_loop(0, slot, add, jnp.zeros((modes, LANES), jnp.float32))
        if pair == 2:
            within = jnp.exp(-pace * float(rows)) * earlier + inner[c].astype(jnp.float32)
            earlier = jnp.where(odd, within, earlier)
        carry[c] = earlier
        hops[c] = jnp.exp(-pace * float(SUB))

    @pl.loop(0, blocks)
    def _(c):
        carried_in(c)

    @pl.when(me < n - 1)
    def _():
        for i in range(6):
            halo_copy(i).wait_send()

    if pair == 2:
        @pl.when(lax.rem(me, 2) == 0)
        def _():
            pair_copy().wait_send()

    @pl.when(leads)
    def _():
        @pl.loop(me + 1, n)
        def _(target):
            state_copy(slot, target).wait_send()


def finish(se, partial, gates, terms, starts, shift, carry, hops, se_out, li_out, made, full, sems):
    blocks, rows = partial.shape[0], partial.shape[1]
    chunks, modes = starts.shape[1], starts.shape[2]
    parts = sems.shape[0] - 1
    each = made.shape[1] // parts
    whole = pltpu.make_async_copy(se, se_out, sems.at[parts])
    whole.start()

    def far(c):
        earlier = carry[c]
        hop = hops[c]
        for a in range(chunks):
            full[a] = starts[c, a] + earlier
            earlier = hop * earlier
            if a == 0:
                earlier = earlier + shift[c]
        cols = pl.ds(pl.multiple_of(c * LANES, LANES), LANES)
        for top in range(0, chunks, SUB):
            span = range(top, min(top + SUB, chunks))
            totals = [partial[c, pl.ds(a * SUB, SUB)] for a in span]
            for m in range(modes):
                term = terms[c, m]
                totals = [total + term * full[a, pl.ds(m, 1)] for a, total in zip(span, totals)]
            first = pl.ds(top * SUB, len(span) * SUB)
            made[first, cols] = (gates[c, first] * jnp.concatenate(totals)).astype(jnp.bfloat16)

    def piece(part):
        cols = pl.ds(part * each, each)
        return pltpu.make_async_copy(made.at[:, cols], li_out.at[:, cols], sems.at[part])

    for part in range(parts):
        @pl.loop(part * (blocks // parts), (part + 1) * (blocks // parts))
        def _(c):
            far(c)

        piece(part).start()
    for part in range(parts):
        piece(part).wait()
    whole.wait()


def shards(*args):
    rows, width = args[0].shape
    modes = args[10].shape[0]
    n, chips = lax.axis_size(GROUP), lax.axis_size("chip")
    blocks, chunks = width // LANES, rows // SUB
    f32 = jnp.float32
    far = pl.BlockSpec(memory_space=pltpu.HBM)
    local = pl.BlockSpec(memory_space=pltpu.VMEM)
    operands = args[:11] + (args[11][None],)
    words = rows * width * 10 + width * modes * (3 * chunks + 3 * SUB + 8 + n)
    budget = min(4 * words + 8 * 2**20, 60 * 2**20)
    parts = 4 if blocks % 4 == 0 else 1
    passed = ((rows, width), jnp.bfloat16), *(((blocks, *shape, LANES), f32) for shape in ((rows,), (rows,), (modes, SUB), (chunks, modes), (modes,), (modes,), (modes,)))
    mixed = pl.pallas_call(
        functools.partial(mixer, n, chips),
        out_shape=tuple(jax.ShapeDtypeStruct(*one) for one in passed),
        in_specs=[far] * 12,
        out_specs=(local,) * len(passed),
        scratch_shapes=[
            pltpu.VMEM((6, rows, width), jnp.bfloat16),
            pltpu.VMEM((6, SUB, width), jnp.bfloat16),
            pltpu.VMEM((n, blocks, modes, LANES), LINK),
            pltpu.VMEM((blocks, modes, LANES), LINK),
            pltpu.VMEM((8, rows + 2 * SUB, LANES), f32),
            pltpu.VMEM((rows + SUB, LANES), f32),
            pltpu.VMEM((blocks, rows + SUB, LANES), f32),
            pltpu.VMEM((blocks, SUB, SUB, LANES), f32),
            pltpu.VMEM((blocks, modes, LANES), f32),
            pltpu.VMEM((blocks, modes, LANES), f32),
            pltpu.VMEM((blocks, modes, LANES), LINK),
            *[pltpu.VMEM(array.shape, f32) for array in operands[6:]],
            pltpu.SemaphoreType.DMA((4,)),
            pltpu.SemaphoreType.DMA((2, parts)),
            pltpu.SemaphoreType.DMA((6,)),
            pltpu.SemaphoreType.DMA((6,)),
            pltpu.SemaphoreType.DMA((6,)),
            pltpu.SemaphoreType.DMA((1,)),
            pltpu.SemaphoreType.DMA((1,)),
            pltpu.SemaphoreType.DMA((n,)),
            pltpu.SemaphoreType.DMA((n,)),
            pltpu.SemaphoreType.REGULAR,
        ],
        compiler_params=pltpu.CompilerParams(collective_id=0, has_side_effects=True, vmem_limit_bytes=budget),
        name="mixer",
    )(*(pltpu.with_memory_space_constraint(array, pltpu.HBM) for array in operands))
    return pl.pallas_call(
        finish,
        out_shape=(jax.ShapeDtypeStruct((rows, width), jnp.bfloat16),) * 2,
        in_specs=[local] * len(passed),
        out_specs=(far, far),
        scratch_shapes=[
            pltpu.VMEM((rows, width), jnp.bfloat16),
            pltpu.VMEM((chunks, modes, LANES), f32),
            pltpu.SemaphoreType.DMA((parts + 1,)),
        ],
        compiler_params=pltpu.CompilerParams(vmem_limit_bytes=8 * 2**20),
        name="finish",
    )(*mixed)


def solution(mesh):
    placed = (P(("dp", "node", "chip"), None),) * 6 + (P(),) * 6
    return jax.shard_map(
        shards,
        mesh=mesh,
        in_specs=placed,
        out_specs=(P(("dp", "node", "chip"), None), P(("dp", "node", "chip"), None)),
        check_vma=False,
    )
```

```python
import functools

import jax
import jax.numpy as jnp
from jax import lax
from jax.experimental import pallas as pl
from jax.experimental.pallas import tpu as pltpu
from jax.sharding import PartitionSpec as P

LANES = 128
SUB = 8
LINK = jnp.bfloat16
GROUP = ("node", "chip")


def paired(n, blocks):
    return n % 2 == 0 and blocks % 2 == 0


def far(c, partial, gates, terms, starts, shift, carry, hops, made, full):
    chunks, modes = starts.shape[1], starts.shape[2]
    earlier = carry[c]
    hop = hops[c]
    for a in range(chunks):
        full[a] = starts[c, a] + earlier
        earlier = hop * earlier
        if a == 0:
            earlier = earlier + shift[c]
    cols = pl.ds(pl.multiple_of(c * LANES, LANES), LANES)
    for top in range(0, chunks, SUB):
        span = range(top, min(top + SUB, chunks))
        totals = [partial[c, pl.ds(a * SUB, SUB)] for a in span]
        for m in range(modes):
            term = terms[c, m]
            totals = [total + term * full[a, pl.ds(m, 1)] for a, total in zip(span, totals)]
        first = pl.ds(top * SUB, len(span) * SUB)
        made[first, cols] = (gates[c, first] * jnp.concatenate(totals)).astype(jnp.bfloat16)


def mixer(n, chips, *refs):
    streams, kept = refs[:6], refs[6:12]
    se, made, partial, gates, terms, starts, shift, carry, hops = refs[12:21]
    (
        held, halo, arrived, sent, ext, extended, u_li, near, carried, own, inner, tally, lent, full,
        se_feature, se_filter, li_feature, residue, rate, skip, in_sem, part_sem, fixed_sem, halo_send, halo_recv, pair_send, pair_recv, state_send, state_recv, swap_send, swap_recv, ready_sem,
    ) = refs[21:]
    rows, width = held.shape[1], held.shape[2]
    blocks = width // LANES
    chunks = rows // SUB
    modes = rate.shape[0]
    lags = se_filter.shape[0]
    pair = 2 if paired(n, blocks) else 1
    half = blocks // pair
    dp = lax.axis_index("dp")
    me = lax.axis_index("node") * chips + lax.axis_index("chip")

    def device(index):
        return (dp, lax.div(index, chips), lax.rem(index, chips))

    order = (4, 5, 1, 2, 0, 3)
    parts = part_sem.shape[1]
    each = width // parts
    loads = [pltpu.make_async_copy(streams[i], held.at[i], in_sem.at[i]) for i in range(4)]

    def piece(i, part):
        cols = pl.ds(part * each, each)
        return pltpu.make_async_copy(streams[i].at[:, cols], held.at[i, :, cols], part_sem.at[i - 4, part])

    fixed = (se_feature, se_filter, li_feature, residue, rate, skip)
    fixed_loads = [pltpu.make_async_copy(kept[i], fixed[i], fixed_sem.at[i]) for i in range(6)]
    for i in (4, 2):
        fixed_loads[i].start()
    for part in range(parts):
        for i in (4, 5):
            piece(i, part).start()

    barrier = pltpu.get_barrier_semaphore()

    side = lax.rem(me, pair)
    odd_core = lax.rem(me, 2) == 1

    def hail(semaphore, other):
        pl.semaphore_signal(semaphore, inc=1, device_id=device(other), device_id_type=pl.DeviceIdType.MESH)

    def hail_if(condition, semaphore, other):
        @pl.when(condition)
        def _():
            hail(semaphore, other)

    if pair == 2:
        hail_if(me > 0, barrier, me - 1)
        hail_if(jnp.logical_not(odd_core), barrier, me + 1)
        hail_if(odd_core & (me > 1), barrier, me - 2)
        hail_if(odd_core & (me < n - 1), barrier, me + 2)
    else:
        @pl.loop(0, n)
        def _(other):
            hail_if(other != me, barrier, other)

    def meet():
        if pair == 2:
            pl.semaphore_wait(barrier, jnp.where(odd_core, 1 + 2 * (me < n - 1).astype(jnp.int32) + (me > 1).astype(jnp.int32), 1))
            if n > 4:
                hail_if(me == n - 3, ready_sem, me - 2)
        else:
            pl.semaphore_wait(barrier, n - 1)

    for i in range(6):
        ext[i, pl.ds(0, 2 * SUB)] = jnp.zeros((2 * SUB, LANES), jnp.float32)

    def columns(c):
        return pl.ds(pl.multiple_of(c * LANES, LANES), LANES)

    def featurized(i, c, taps, stream, early):
        cols = columns(c)
        if i not in (4, 5):
            ext[i, pl.ds(SUB, SUB)] = halo[i, :, cols].astype(jnp.float32)
        ext[i, pl.ds(2 * SUB, rows)] = held[i, :, cols].astype(jnp.float32)
        first, count = 2 * SUB - early, rows + early
        total = taps[0, pl.ds(stream, 1), cols] * ext[i, pl.ds(first, count)]
        for lag in (1, 2):
            total = total + taps[lag, pl.ds(stream, 1), cols] * ext[i, pl.ds(first - lag, count)]
        return total

    def local_states(c):
        cols = columns(c)
        product = featurized(4, c, li_feature, 1, 0) * featurized(5, c, li_feature, 2, 0)
        u_li[c, pl.ds(0, SUB)] = jnp.zeros((SUB, LANES), jnp.float32)
        u_li[c, pl.ds(SUB, rows)] = product.astype(jnp.bfloat16).astype(jnp.float32)
        pace = rate[:, cols]
        powers = [None] + [jnp.exp(-pace * float(k)) for k in range(1, SUB + 1)]
        state = jnp.zeros((modes, LANES), jnp.float32)
        for a in range(chunks):
            starts[c, a] = state
            new = jnp.broadcast_to(u_li[c, pl.ds(SUB + a * SUB + SUB - 1, 1)], (modes, LANES))
            for b in range(SUB - 1):
                new = new + powers[SUB - 1 - b] * u_li[c, pl.ds(SUB + a * SUB + b, 1)]
            state = powers[SUB] * state + new
        own[c] = state

    tail = (2, SUB, SUB, 2, 2, 2)

    def halo_copy(i):
        return pltpu.make_async_remote_copy(
            src_ref=streams[i].at[pl.ds(rows - tail[i], tail[i])],
            dst_ref=halo.at[i, pl.ds(SUB - tail[i], tail[i])],
            send_sem=halo_send.at[i],
            recv_sem=halo_recv.at[i],
            device_id=device(lax.rem(me + 1, n)),
            device_id_type=pl.DeviceIdType.MESH,
        )

    per = blocks // parts

    def states(first, last):
        @pl.loop(first, last)
        def _(c):
            local_states(c)

    for i in (4, 2):
        fixed_loads[i].wait()
    for part in range(parts):
        for i in (4, 5):
            piece(i, part).wait()
        if part == 0:
            for i in (3, 5, 0, 1):
                fixed_loads[i].start()
            for i in (1, 2, 0, 3):
                loads[i].start()
            states(0, per // 2)
            meet()

            @pl.when(me < n - 1)
            def _():
                for i in order:
                    halo_copy(i).start()

            states(per // 2, per)
        else:
            states(part * per, (part + 1) * per)

    if pair == 2:
        @pl.when(odd_core & (me > 1) & (me < n - 4))
        def _():
            pl.semaphore_wait(ready_sem, 1)
            hail(ready_sem, me - 2)

    @pl.when(me == 0)
    def _():
        halo[...] = jnp.zeros_like(halo)

    if pair == 2:
        @pl.when(lax.rem(me, 2) == 0)
        def _():
            inner[...] = jnp.zeros_like(inner)


    place = lax.broadcasted_iota(jnp.int32, (SUB, LANES), 0)
    step = place.astype(jnp.float32)

    def ready(i):
        @pl.when(me > 0)
        def _():
            halo_copy(i).wait_recv()

    ready(4)
    ready(5)

    wide = 4 if blocks % 4 == 0 else 1

    def fixed_up(c, j):
        cols = columns(c)

        def opening(i, stream):
            at = 2 * j + i - 4
            ext[at, pl.ds(SUB, SUB)] = halo[i, :, cols].astype(jnp.float32)
            ext[at, pl.ds(2 * SUB, SUB)] = held[i, pl.ds(0, SUB), cols].astype(jnp.float32)
            total = li_feature[0, pl.ds(stream, 1), cols] * ext[at, pl.ds(2 * SUB, SUB)]
            for lag in (1, 2):
                total = total + li_feature[lag, pl.ds(stream, 1), cols] * ext[at, pl.ds(2 * SUB - lag, SUB)]
            return total

        right = (opening(4, 1) * opening(5, 2)).astype(jnp.bfloat16).astype(jnp.float32)
        extended[pl.ds(j * SUB, SUB)] = right - u_li[c, pl.ds(SUB, SUB)]
        u_li[c, pl.ds(SUB, SUB)] = right
        pace = rate[:, cols]
        moved = jnp.exp(-pace * float(SUB - 1)) * extended[pl.ds(j * SUB, 1)]
        moved = moved + jnp.exp(-pace * float(SUB - 2)) * extended[pl.ds(j * SUB + 1, 1)]
        shift[c] = moved
        state = own[c] + jnp.exp(-pace * float(rows - SUB)) * moved
        own[c] = state
        sent[c] = state.astype(sent.dtype)

    @pl.loop(0, blocks // wide)
    def _(many):
        for j in range(wide):
            fixed_up(many * wide + j, j)

    def state_copy(source, target):
        return pltpu.make_async_remote_copy(
            src_ref=sent.at[pl.ds(lax.rem(target, pair) * half, half)],
            dst_ref=arrived.at[source, pl.ds(lax.rem(target, pair) * half, half)],
            send_sem=state_send.at[target],
            recv_sem=state_recv.at[source],
            device_id=device(target),
            device_id_type=pl.DeviceIdType.MESH,
        )

    def pair_copy():
        return pltpu.make_async_remote_copy(
            src_ref=sent,
            dst_ref=inner,
            send_sem=pair_send.at[0],
            recv_sem=pair_recv.at[0],
            device_id=device(me + 1 - 2 * lax.rem(me, 2)),
            device_id_type=pl.DeviceIdType.MESH,
        )

    if pair == 2:
        @pl.when(lax.rem(me, 2) == 0)
        def _():
            pair_copy().start()

    for i in (3, 5, 0, 1):
        fixed_loads[i].wait()

    @pl.loop(0, blocks)
    def _(c):
        cols = columns(c)
        pace = rate[:, cols]
        twice = 2.0 * pace
        small = twice * (1.0 - twice * (0.5 - twice * (1.0 / 6.0 - twice * (1.0 / 24.0 - twice * (1.0 / 120.0)))))
        gap = jnp.where(twice < 0.03125, small, 1.0 - jnp.exp(-twice))
        carried[c] = residue[:, cols] * jnp.sqrt(gap)
        hops[c] = jnp.exp(-pace * float(SUB))
        total = jnp.zeros((SUB, LANES), jnp.float32)
        for m in range(modes):
            speed = rate[pl.ds(m, 1), cols]
            term = carried[c, pl.ds(m, 1)] * jnp.exp(-speed * step)
            total = total + term
            terms[c, m] = term * jnp.exp(-speed)
        near[c, 0] = total
        for lag in range(SUB - 1, -1, -1):
            tap = near[c, 0, pl.ds(lag, 1)]
            if lag == 0:
                tap = tap + skip[:, cols]
            near[c, lag] = jnp.where(place >= lag, jnp.broadcast_to(tap, (SUB, LANES)), 0.0)

    if pair == 2:
        @pl.when(lax.rem(me, 2) == 1)
        def _():
            pair_copy().wait_recv()

            @pl.loop(0, blocks)
            def _(c):
                fall = jnp.exp(-rate[:, columns(c)] * float(rows))
                sent[c] = (fall * inner[c].astype(jnp.float32) + own[c]).astype(sent.dtype)

    leads = lax.rem(me, pair) == pair - 1
    slot = lax.div(me, pair)

    def send_states(first, last):
        @pl.when(leads)
        def _():
            @pl.loop(first, last)
            def _(target):
                state_copy(slot, target).start()

    if pair == 2:
        send_states(me + 1, jnp.minimum(me + 3, n))

        if n > 4:
            @pl.when(me == 1)
            def _():
                pl.semaphore_wait(ready_sem, 1)

        send_states(me + 3, n)
    else:
        send_states(me + 1, n)

    for i in (1, 2, 0, 3):
        loads[i].wait()
        ready(i)

    @pl.loop(0, blocks)
    def _(c):
        cols = columns(c)
        product = featurized(1, c, se_feature, 1, SUB) * featurized(2, c, se_feature, 2, SUB)
        extended[...] = product.astype(jnp.bfloat16).astype(jnp.float32)
        mixed = se_filter[pl.ds(0, 1), cols] * extended[pl.ds(SUB, rows)]
        for lag in range(1, lags):
            mixed = mixed + se_filter[pl.ds(lag, 1), cols] * extended[pl.ds(SUB - lag, rows)]
        se[:, cols] = (featurized(0, c, se_feature, 0, 0) * mixed).astype(jnp.bfloat16)
        gates[c] = featurized(3, c, li_feature, 0, 0)
        taps = [near[c, lag] for lag in range(SUB)]
        for a in range(chunks):
            total = taps[0] * u_li[c, pl.ds(SUB + a * SUB, SUB)]
            for lag in range(1, SUB):
                total = total + taps[lag] * u_li[c, pl.ds(SUB + a * SUB - lag, SUB)]
            partial[c, pl.ds(a * SUB, SUB)] = total

    odd = lax.rem(jnp.full((modes, LANES), me, jnp.int32), 2) == 1
    step_by = 4 if half % 4 == 0 else 1

    def by_four(first, body):
        @pl.loop(0, half // step_by)
        def _(many):
            for j in range(step_by):
                body(first + many * step_by + j)

    def cleared(c):
        tally[c] = jnp.zeros((modes, LANES), jnp.float32)

    def summed(source):
        def body(c):
            fall = jnp.exp(-rate[:, columns(c)] * float(rows * pair))
            tally[c] = fall * tally[c] + arrived[source, c].astype(jnp.float32)

        return body

    def lend(c):
        lent[c] = tally[c].astype(lent.dtype)

    def carried_in(c, before):
        if pair == 2:
            within = jnp.exp(-rate[:, columns(c)] * float(rows)) * before + inner[c].astype(jnp.float32)
            before = jnp.where(odd, within, before)
        carry[c] = before

    ours, theirs = side * half, (pair - 1 - side) * half
    by_four(ours, cleared)

    @pl.loop(0, slot)
    def _(source):
        state_copy(source, me).wait_recv()
        by_four(ours, summed(source))

    def swap_copy(first):
        return pltpu.make_async_remote_copy(
            src_ref=lent.at[pl.ds(first, half)],
            dst_ref=lent.at[pl.ds(first, half)],
            send_sem=swap_send.at[0],
            recv_sem=swap_recv.at[0],
            device_id=device(me + 1 - 2 * lax.rem(me, 2)),
            device_id_type=pl.DeviceIdType.MESH,
        )

    if pair == 2:
        @pl.when(slot > 0)
        def _():
            by_four(ours, lend)
            swap_copy(ours).start()

        @pl.when(slot == 0)
        def _():
            lent[...] = jnp.zeros_like(lent)

    by_four(ours, lambda c: carried_in(c, tally[c]))

    @pl.loop(0, half)
    def _(c):
        far(ours + c, partial, gates, terms, starts, shift, carry, hops, made, full)

    if pair == 2:
        @pl.when(slot > 0)
        def _():
            swap_copy(theirs).wait_recv()

        by_four(theirs, lambda c: carried_in(c, lent[c].astype(jnp.float32)))

        @pl.when(slot > 0)
        def _():
            swap_copy(ours).wait_send()

    @pl.when(me < n - 1)
    def _():
        for i in range(6):
            halo_copy(i).wait_send()

    if pair == 2:
        @pl.when(lax.rem(me, 2) == 0)
        def _():
            pair_copy().wait_send()

    @pl.when(leads)
    def _():
        @pl.loop(me + 1, n)
        def _(target):
            state_copy(slot, target).wait_send()


def finish(n, chips, se, made, partial, gates, terms, starts, shift, carry, hops, se_out, li_out, rest, full, sems):
    blocks = partial.shape[0]
    width = se.shape[1]
    pair = 2 if paired(n, blocks) else 1
    half = blocks // pair
    me = lax.axis_index("node") * chips + lax.axis_index("chip")
    ours = lax.rem(me, pair) * half
    theirs = half - ours

    def columns(first, count):
        return pl.ds(pl.multiple_of(first * LANES, LANES), count * LANES)

    own = columns(ours, half)
    done = [pltpu.make_async_copy(se, se_out, sems.at[0]), pltpu.make_async_copy(made.at[:, own], li_out.at[:, own], sems.at[1])]
    for copy in done:
        copy.start()
    if pair == 2:
        parts = sems.shape[0] - 2
        each = half // parts
        for part in range(parts):
            @pl.loop(part * each, (part + 1) * each)
            def _(c):
                far(theirs + c, partial, gates, terms, starts, shift, carry, hops, rest, full)

            cols = columns(theirs + part * each, each)
            done.append(pltpu.make_async_copy(rest.at[:, cols], li_out.at[:, cols], sems.at[2 + part]))
            done[-1].start()
    for copy in done:
        copy.wait()


def shards(*args):
    rows, width = args[0].shape
    modes = args[10].shape[0]
    n, chips = lax.axis_size(GROUP), lax.axis_size("chip")
    blocks, chunks = width // LANES, rows // SUB
    f32 = jnp.float32
    far = pl.BlockSpec(memory_space=pltpu.HBM)
    local = pl.BlockSpec(memory_space=pltpu.VMEM)
    operands = args[:11] + (args[11][None],)
    words = rows * width * 10 + width * modes * (3 * chunks + 3 * SUB + 8 + n)
    budget = min(4 * words + 8 * 2**20, 60 * 2**20)
    parts = 4 if blocks % 4 == 0 else 1
    passed = ((rows, width), jnp.bfloat16), ((rows, width), jnp.bfloat16), *(((blocks, *shape, LANES), f32) for shape in ((rows,), (rows,), (modes, SUB), (chunks, modes), (modes,), (modes,), (modes,)))
    mixed = pl.pallas_call(
        functools.partial(mixer, n, chips),
        out_shape=tuple(jax.ShapeDtypeStruct(*one) for one in passed),
        in_specs=[far] * 12,
        out_specs=(local,) * len(passed),
        scratch_shapes=[
            pltpu.VMEM((6, rows, width), jnp.bfloat16),
            pltpu.VMEM((6, SUB, width), jnp.bfloat16),
            pltpu.VMEM((n, blocks, modes, LANES), LINK),
            pltpu.VMEM((blocks, modes, LANES), LINK),
            pltpu.VMEM((8, rows + 2 * SUB, LANES), f32),
            pltpu.VMEM((rows + SUB, LANES), f32),
            pltpu.VMEM((blocks, rows + SUB, LANES), f32),
            pltpu.VMEM((blocks, SUB, SUB, LANES), f32),
            pltpu.VMEM((blocks, modes, LANES), f32),
            pltpu.VMEM((blocks, modes, LANES), f32),
            pltpu.VMEM((blocks, modes, LANES), LINK),
            pltpu.VMEM((blocks, modes, LANES), f32),
            pltpu.VMEM((blocks, modes, LANES), LINK),
            pltpu.VMEM((chunks, modes, LANES), f32),
            *[pltpu.VMEM(array.shape, f32) for array in operands[6:]],
            pltpu.SemaphoreType.DMA((4,)),
            pltpu.SemaphoreType.DMA((2, parts)),
            pltpu.SemaphoreType.DMA((6,)),
            pltpu.SemaphoreType.DMA((6,)),
            pltpu.SemaphoreType.DMA((6,)),
            pltpu.SemaphoreType.DMA((1,)),
            pltpu.SemaphoreType.DMA((1,)),
            pltpu.SemaphoreType.DMA((n,)),
            pltpu.SemaphoreType.DMA((n,)),
            pltpu.SemaphoreType.DMA((1,)),
            pltpu.SemaphoreType.DMA((1,)),
            pltpu.SemaphoreType.REGULAR,
        ],
        compiler_params=pltpu.CompilerParams(collective_id=0, has_side_effects=True, vmem_limit_bytes=budget),
        name="mixer",
    )(*(pltpu.with_memory_space_constraint(array, pltpu.HBM) for array in operands))
    return pl.pallas_call(
        functools.partial(finish, n, chips),
        out_shape=(jax.ShapeDtypeStruct((rows, width), jnp.bfloat16),) * 2,
        in_specs=[local] * len(passed),
        out_specs=(far, far),
        scratch_shapes=[
            pltpu.VMEM((rows, width), jnp.bfloat16),
            pltpu.VMEM((chunks, modes, LANES), f32),
            pltpu.SemaphoreType.DMA((2 + (2 if blocks % 4 == 0 else 1),)),
        ],
        compiler_params=pltpu.CompilerParams(vmem_limit_bytes=8 * 2**20),
        name="finish",
    )(*mixed)


def solution(mesh):
    placed = (P(("dp", "node", "chip"), None),) * 6 + (P(),) * 6
    return jax.shard_map(
        shards,
        mesh=mesh,
        in_specs=placed,
        out_specs=(P(("dp", "node", "chip"), None), P(("dp", "node", "chip"), None)),
        check_vma=False,
    )
```

```python
import functools

import jax
import jax.numpy as jnp
from jax import lax
from jax.experimental import pallas as pl
from jax.experimental.pallas import tpu as pltpu
from jax.sharding import PartitionSpec as P

LANES = 128
SUB = 8
LINK = jnp.bfloat16
GROUP = ("node", "chip")


def paired(n, blocks):
    return n % 2 == 0 and blocks % 2 == 0


def far(c, partial, gates, terms, starts, shift, carry, hops, made, full):
    chunks, modes = starts.shape[1], starts.shape[2]
    earlier = carry[c]
    hop = hops[c]
    for a in range(chunks):
        full[a] = starts[c, a] + earlier
        earlier = hop * earlier
        if a == 0:
            earlier = earlier + shift[c]
    cols = pl.ds(pl.multiple_of(c * LANES, LANES), LANES)
    for top in range(0, chunks, SUB):
        span = range(top, min(top + SUB, chunks))
        totals = [partial[c, pl.ds(a * SUB, SUB)] for a in span]
        for m in range(modes):
            term = terms[c, m]
            totals = [total + term * full[a, pl.ds(m, 1)] for a, total in zip(span, totals)]
        first = pl.ds(top * SUB, len(span) * SUB)
        made[first, cols] = (gates[c, first] * jnp.concatenate(totals)).astype(jnp.bfloat16)


def mixer(n, chips, *refs):
    streams, kept = refs[:6], refs[6:12]
    se, made, partial, gates, terms, starts, shift, carry, hops = refs[12:21]
    (
        held, halo, arrived, sent, ext, extended, u_li, near, hold, own, inner, tally, lent, full,
        se_feature, se_filter, li_feature, residue, rate, skip, in_sem, part_sem, fixed_sem, halo_send, halo_recv, pair_send, pair_recv, state_send, state_recv, swap_send, swap_recv, ready_sem,
    ) = refs[21:]
    rows, width = held.shape[1], held.shape[2]
    blocks = width // LANES
    chunks = rows // SUB
    modes = rate.shape[0]
    lags = se_filter.shape[0]
    pair = 2 if paired(n, blocks) else 1
    half = blocks // pair
    dp = lax.axis_index("dp")
    me = lax.axis_index("node") * chips + lax.axis_index("chip")

    def device(index):
        return (dp, lax.div(index, chips), lax.rem(index, chips))

    order = (4, 5, 3, 1, 2, 0)
    parts = part_sem.shape[1]
    each = width // parts
    loads = [pltpu.make_async_copy(streams[i], held.at[i], in_sem.at[i]) for i in range(4)]

    def piece(i, part):
        cols = pl.ds(part * each, each)
        return pltpu.make_async_copy(streams[i].at[:, cols], held.at[i, :, cols], part_sem.at[i - 4, part])

    fixed = (se_feature, se_filter, li_feature, residue, rate, skip)
    fixed_loads = [pltpu.make_async_copy(kept[i], fixed[i], fixed_sem.at[i]) for i in range(6)]
    for i in (4, 2):
        fixed_loads[i].start()
    for part in range(parts):
        for i in (4, 5):
            piece(i, part).start()

    barrier = pltpu.get_barrier_semaphore()

    side = lax.rem(me, pair)
    odd_core = lax.rem(me, 2) == 1

    def hail(semaphore, other):
        pl.semaphore_signal(semaphore, inc=1, device_id=device(other), device_id_type=pl.DeviceIdType.MESH)

    def hail_if(condition, semaphore, other):
        @pl.when(condition)
        def _():
            hail(semaphore, other)

    if pair == 2:
        hail_if(me > 0, barrier, me - 1)
        hail_if(jnp.logical_not(odd_core), barrier, me + 1)
        hail_if(odd_core & (me > 1), barrier, me - 2)
        hail_if(odd_core & (me < n - 1), barrier, me + 2)
    else:
        @pl.loop(0, n)
        def _(other):
            hail_if(other != me, barrier, other)

    def meet():
        if pair == 2:
            pl.semaphore_wait(barrier, jnp.where(odd_core, 1 + 2 * (me < n - 1).astype(jnp.int32) + (me > 1).astype(jnp.int32), 1))
            if n > 4:
                hail_if(me == n - 3, ready_sem, me - 2)
        else:
            pl.semaphore_wait(barrier, n - 1)

    for i in range(6):
        ext[i, pl.ds(0, 2 * SUB)] = jnp.zeros((2 * SUB, LANES), jnp.float32)

    def columns(c):
        return pl.ds(pl.multiple_of(c * LANES, LANES), LANES)

    def featurized(i, c, taps, stream, early):
        cols = columns(c)
        if i not in (4, 5):
            ext[i, pl.ds(SUB, SUB)] = halo[i, :, cols].astype(jnp.float32)
        ext[i, pl.ds(2 * SUB, rows)] = held[i, :, cols].astype(jnp.float32)
        first, count = 2 * SUB - early, rows + early
        total = taps[0, pl.ds(stream, 1), cols] * ext[i, pl.ds(first, count)]
        for lag in (1, 2):
            total = total + taps[lag, pl.ds(stream, 1), cols] * ext[i, pl.ds(first - lag, count)]
        return total

    def local_states(c):
        cols = columns(c)
        product = featurized(4, c, li_feature, 1, 0) * featurized(5, c, li_feature, 2, 0)
        u_li[c, pl.ds(0, SUB)] = jnp.zeros((SUB, LANES), jnp.float32)
        u_li[c, pl.ds(SUB, rows)] = product.astype(jnp.bfloat16).astype(jnp.float32)
        pace = rate[:, cols]
        powers = [None] + [jnp.exp(-pace * float(k)) for k in range(1, SUB + 1)]
        state = jnp.zeros((modes, LANES), jnp.float32)
        for a in range(chunks):
            starts[c, a] = state
            new = jnp.broadcast_to(u_li[c, pl.ds(SUB + a * SUB + SUB - 1, 1)], (modes, LANES))
            for b in range(SUB - 1):
                new = new + powers[SUB - 1 - b] * u_li[c, pl.ds(SUB + a * SUB + b, 1)]
            state = powers[SUB] * state + new
        own[c] = state

    tail = (2, SUB, SUB, 2, 2, 2)

    def halo_copy(i):
        return pltpu.make_async_remote_copy(
            src_ref=streams[i].at[pl.ds(rows - tail[i], tail[i])],
            dst_ref=halo.at[i, pl.ds(SUB - tail[i], tail[i])],
            send_sem=halo_send.at[i],
            recv_sem=halo_recv.at[i],
            device_id=device(lax.rem(me + 1, n)),
            device_id_type=pl.DeviceIdType.MESH,
        )

    per = blocks // parts

    def states(first, last):
        @pl.loop(first, last)
        def _(c):
            local_states(c)

    for i in (4, 2):
        fixed_loads[i].wait()
    for part in range(parts):
        for i in (4, 5):
            piece(i, part).wait()
        if part == 0:
            for i in (3, 5, 0, 1):
                fixed_loads[i].start()
            for i in (3, 1, 2, 0):
                loads[i].start()
            states(0, per // 2)
            meet()

            @pl.when(me < n - 1)
            def _():
                for i in order:
                    halo_copy(i).start()

            states(per // 2, per)
        else:
            states(part * per, (part + 1) * per)

    if pair == 2:
        @pl.when(odd_core & (me > 1) & (me < n - 4))
        def _():
            pl.semaphore_wait(ready_sem, 1)
            hail(ready_sem, me - 2)

    @pl.when(me == 0)
    def _():
        halo[...] = jnp.zeros_like(halo)

    if pair == 2:
        @pl.when(lax.rem(me, 2) == 0)
        def _():
            inner[...] = jnp.zeros_like(inner)


    place = lax.broadcasted_iota(jnp.int32, (SUB, LANES), 0)
    step = place.astype(jnp.float32)

    def ready(i):
        @pl.when(me > 0)
        def _():
            halo_copy(i).wait_recv()

    def state_copy(source, target):
        return pltpu.make_async_remote_copy(
            src_ref=sent.at[pl.ds(lax.rem(target, pair) * half, half)],
            dst_ref=arrived.at[source, pl.ds(lax.rem(target, pair) * half, half)],
            send_sem=state_send.at[target],
            recv_sem=state_recv.at[source],
            device_id=device(target),
            device_id_type=pl.DeviceIdType.MESH,
        )

    def pair_copy():
        return pltpu.make_async_remote_copy(
            src_ref=sent,
            dst_ref=inner,
            send_sem=pair_send.at[0],
            recv_sem=pair_recv.at[0],
            device_id=device(me + 1 - 2 * lax.rem(me, 2)),
            device_id_type=pl.DeviceIdType.MESH,
        )

    for i in (3, 5, 0, 1):
        fixed_loads[i].wait()

    backward = -step

    def filters(c, j):
        cols = columns(c)
        pace = rate[:, cols]
        twice = 2.0 * pace
        small = twice * (1.0 - twice * (0.5 - twice * (1.0 / 6.0 - twice * (1.0 / 24.0 - twice * (1.0 / 120.0)))))
        gap = jnp.where(twice < 0.03125, small, 1.0 - jnp.exp(-twice))
        rows_of = hold.at[j]
        rows_of[pl.ds(0, modes)] = residue[:, cols] * jnp.sqrt(gap)
        rows_of[pl.ds(modes, modes)] = jnp.exp(-pace)
        hops[c] = jnp.exp(-pace * float(SUB))
        total = jnp.zeros((SUB, LANES), jnp.float32)
        for m in range(modes):
            term = rows_of[pl.ds(m, 1)] * jnp.exp(rate[pl.ds(m, 1), cols] * backward)
            total = total + term
            terms[c, m] = term * rows_of[pl.ds(modes + m, 1)]
        rows_of[pl.ds(2 * modes, SUB)] = total
        for lag in range(SUB):
            tap = rows_of[pl.ds(2 * modes + lag, 1)]
            if lag == 0:
                tap = tap + skip[:, cols]
            near[c, lag] = jnp.where(place >= lag, jnp.broadcast_to(tap, (SUB, LANES)), 0.0)

    twin = hold.shape[0]

    @pl.loop(0, blocks // twin)
    def _(many):
        for j in range(twin):
            filters(many * twin + j, j)

    ready(4)
    ready(5)

    wide = 4 if blocks % 4 == 0 else 1

    def fixed_up(c, j):
        cols = columns(c)

        def opening(i, stream):
            at = 2 * j + i - 4
            ext[at, pl.ds(SUB, SUB)] = halo[i, :, cols].astype(jnp.float32)
            ext[at, pl.ds(2 * SUB, SUB)] = held[i, pl.ds(0, SUB), cols].astype(jnp.float32)
            total = li_feature[0, pl.ds(stream, 1), cols] * ext[at, pl.ds(2 * SUB, SUB)]
            for lag in (1, 2):
                total = total + li_feature[lag, pl.ds(stream, 1), cols] * ext[at, pl.ds(2 * SUB - lag, SUB)]
            return total

        right = (opening(4, 1) * opening(5, 2)).astype(jnp.bfloat16).astype(jnp.float32)
        extended[pl.ds(j * SUB, SUB)] = right - u_li[c, pl.ds(SUB, SUB)]
        u_li[c, pl.ds(SUB, SUB)] = right
        pace = rate[:, cols]
        moved = jnp.exp(-pace * float(SUB - 1)) * extended[pl.ds(j * SUB, 1)]
        moved = moved + jnp.exp(-pace * float(SUB - 2)) * extended[pl.ds(j * SUB + 1, 1)]
        shift[c] = moved
        state = own[c] + jnp.exp(-pace * float(rows - SUB)) * moved
        own[c] = state
        sent[c] = state.astype(sent.dtype)

    @pl.loop(0, blocks // wide)
    def _(many):
        for j in range(wide):
            fixed_up(many * wide + j, j)

    if pair == 2:
        @pl.when(lax.rem(me, 2) == 0)
        def _():
            pair_copy().start()

    loads[3].wait()
    ready(3)

    @pl.loop(0, blocks)
    def _(c):
        gates[c] = featurized(3, c, li_feature, 0, 0)
        taps = [near[c, lag] for lag in range(SUB)]
        for a in range(chunks):
            total = taps[0] * u_li[c, pl.ds(SUB + a * SUB, SUB)]
            for lag in range(1, SUB):
                total = total + taps[lag] * u_li[c, pl.ds(SUB + a * SUB - lag, SUB)]
            partial[c, pl.ds(a * SUB, SUB)] = total

    if pair == 2:
        @pl.when(lax.rem(me, 2) == 1)
        def _():
            pair_copy().wait_recv()

            @pl.loop(0, blocks)
            def _(c):
                fall = jnp.exp(-rate[:, columns(c)] * float(rows))
                sent[c] = (fall * inner[c].astype(jnp.float32) + own[c]).astype(sent.dtype)

    leads = lax.rem(me, pair) == pair - 1
    slot = lax.div(me, pair)

    def send_states(first, last):
        @pl.when(leads)
        def _():
            @pl.loop(first, last)
            def _(target):
                state_copy(slot, target).start()

    if pair == 2:
        send_states(me + 1, jnp.minimum(me + 3, n))

        if n > 4:
            @pl.when(me == 1)
            def _():
                pl.semaphore_wait(ready_sem, 1)

        send_states(me + 3, n)
    else:
        send_states(me + 1, n)

    for i in (1, 2, 0):
        loads[i].wait()
        ready(i)

    @pl.loop(0, blocks)
    def _(c):
        cols = columns(c)
        product = featurized(1, c, se_feature, 1, SUB) * featurized(2, c, se_feature, 2, SUB)
        extended[...] = product.astype(jnp.bfloat16).astype(jnp.float32)
        mixed = se_filter[pl.ds(0, 1), cols] * extended[pl.ds(SUB, rows)]
        for lag in range(1, lags):
            mixed = mixed + se_filter[pl.ds(lag, 1), cols] * extended[pl.ds(SUB - lag, rows)]
        se[:, cols] = (featurized(0, c, se_feature, 0, 0) * mixed).astype(jnp.bfloat16)

    odd = lax.rem(jnp.full((modes, LANES), me, jnp.int32), 2) == 1
    step_by = 4 if half % 4 == 0 else 1

    def by_four(first, body):
        @pl.loop(0, half // step_by)
        def _(many):
            for j in range(step_by):
                body(first + many * step_by + j)

    def cleared(c):
        tally[c] = jnp.zeros((modes, LANES), jnp.float32)

    def summed(source):
        def body(c):
            fall = jnp.exp(-rate[:, columns(c)] * float(rows * pair))
            tally[c] = fall * tally[c] + arrived[source, c].astype(jnp.float32)

        return body

    def lend(c):
        lent[c] = tally[c].astype(lent.dtype)

    def carried_in(c, before):
        if pair == 2:
            within = jnp.exp(-rate[:, columns(c)] * float(rows)) * before + inner[c].astype(jnp.float32)
            before = jnp.where(odd, within, before)
        carry[c] = before

    ours, theirs = side * half, (pair - 1 - side) * half
    by_four(ours, cleared)

    @pl.loop(0, slot)
    def _(source):
        state_copy(source, me).wait_recv()
        by_four(ours, summed(source))

    def swap_copy(first):
        return pltpu.make_async_remote_copy(
            src_ref=lent.at[pl.ds(first, half)],
            dst_ref=lent.at[pl.ds(first, half)],
            send_sem=swap_send.at[0],
            recv_sem=swap_recv.at[0],
            device_id=device(me + 1 - 2 * lax.rem(me, 2)),
            device_id_type=pl.DeviceIdType.MESH,
        )

    if pair == 2:
        @pl.when(slot > 0)
        def _():
            by_four(ours, lend)
            swap_copy(ours).start()

        @pl.when(slot == 0)
        def _():
            lent[...] = jnp.zeros_like(lent)

    by_four(ours, lambda c: carried_in(c, tally[c]))

    @pl.loop(0, half)
    def _(c):
        far(ours + c, partial, gates, terms, starts, shift, carry, hops, made, full)

    if pair == 2:
        @pl.when(slot > 0)
        def _():
            swap_copy(theirs).wait_recv()

        by_four(theirs, lambda c: carried_in(c, lent[c].astype(jnp.float32)))

        @pl.when(slot > 0)
        def _():
            swap_copy(ours).wait_send()

    @pl.when(me < n - 1)
    def _():
        for i in range(6):
            halo_copy(i).wait_send()

    if pair == 2:
        @pl.when(lax.rem(me, 2) == 0)
        def _():
            pair_copy().wait_send()

    @pl.when(leads)
    def _():
        @pl.loop(me + 1, n)
        def _(target):
            state_copy(slot, target).wait_send()


def finish(n, chips, se, made, partial, gates, terms, starts, shift, carry, hops, se_out, li_out, rest, full, sems):
    blocks = partial.shape[0]
    width = se.shape[1]
    pair = 2 if paired(n, blocks) else 1
    half = blocks // pair
    me = lax.axis_index("node") * chips + lax.axis_index("chip")
    ours = lax.rem(me, pair) * half
    theirs = half - ours

    def columns(first, count):
        return pl.ds(pl.multiple_of(first * LANES, LANES), count * LANES)

    own = columns(ours, half)
    done = [pltpu.make_async_copy(se, se_out, sems.at[0]), pltpu.make_async_copy(made.at[:, own], li_out.at[:, own], sems.at[1])]
    for copy in done:
        copy.start()
    if pair == 2:
        parts = sems.shape[0] - 2
        each = half // parts
        for part in range(parts):
            @pl.loop(part * each, (part + 1) * each)
            def _(c):
                far(theirs + c, partial, gates, terms, starts, shift, carry, hops, rest, full)

            cols = columns(theirs + part * each, each)
            done.append(pltpu.make_async_copy(rest.at[:, cols], li_out.at[:, cols], sems.at[2 + part]))
            done[-1].start()
    for copy in done:
        copy.wait()


def shards(*args):
    rows, width = args[0].shape
    modes = args[10].shape[0]
    n, chips = lax.axis_size(GROUP), lax.axis_size("chip")
    blocks, chunks = width // LANES, rows // SUB
    f32 = jnp.float32
    far = pl.BlockSpec(memory_space=pltpu.HBM)
    local = pl.BlockSpec(memory_space=pltpu.VMEM)
    operands = args[:11] + (args[11][None],)
    words = rows * width * 10 + width * modes * (3 * chunks + 3 * SUB + 8 + n)
    budget = min(4 * words + 8 * 2**20, 60 * 2**20)
    parts = 4 if blocks % 4 == 0 else 1
    passed = ((rows, width), jnp.bfloat16), ((rows, width), jnp.bfloat16), *(((blocks, *shape, LANES), f32) for shape in ((rows,), (rows,), (modes, SUB), (chunks, modes), (modes,), (modes,), (modes,)))
    mixed = pl.pallas_call(
        functools.partial(mixer, n, chips),
        out_shape=tuple(jax.ShapeDtypeStruct(*one) for one in passed),
        in_specs=[far] * 12,
        out_specs=(local,) * len(passed),
        scratch_shapes=[
            pltpu.VMEM((6, rows, width), jnp.bfloat16),
            pltpu.VMEM((6, SUB, width), jnp.bfloat16),
            pltpu.VMEM((n, blocks, modes, LANES), LINK),
            pltpu.VMEM((blocks, modes, LANES), LINK),
            pltpu.VMEM((8, rows + 2 * SUB, LANES), f32),
            pltpu.VMEM((rows + SUB, LANES), f32),
            pltpu.VMEM((blocks, rows + SUB, LANES), f32),
            pltpu.VMEM((blocks, SUB, SUB, LANES), f32),
            pltpu.VMEM((2 if blocks % 2 == 0 else 1, 2 * modes + SUB, LANES), f32),
            pltpu.VMEM((blocks, modes, LANES), f32),
            pltpu.VMEM((blocks, modes, LANES), LINK),
            pltpu.VMEM((blocks, modes, LANES), f32),
            pltpu.VMEM((blocks, modes, LANES), LINK),
            pltpu.VMEM((chunks, modes, LANES), f32),
            *[pltpu.VMEM(array.shape, f32) for array in operands[6:]],
            pltpu.SemaphoreType.DMA((4,)),
            pltpu.SemaphoreType.DMA((2, parts)),
            pltpu.SemaphoreType.DMA((6,)),
            pltpu.SemaphoreType.DMA((6,)),
            pltpu.SemaphoreType.DMA((6,)),
            pltpu.SemaphoreType.DMA((1,)),
            pltpu.SemaphoreType.DMA((1,)),
            pltpu.SemaphoreType.DMA((n,)),
            pltpu.SemaphoreType.DMA((n,)),
            pltpu.SemaphoreType.DMA((1,)),
            pltpu.SemaphoreType.DMA((1,)),
            pltpu.SemaphoreType.REGULAR,
        ],
        compiler_params=pltpu.CompilerParams(collective_id=0, has_side_effects=True, vmem_limit_bytes=budget),
        name="mixer",
    )(*(pltpu.with_memory_space_constraint(array, pltpu.HBM) for array in operands))
    return pl.pallas_call(
        functools.partial(finish, n, chips),
        out_shape=(jax.ShapeDtypeStruct((rows, width), jnp.bfloat16),) * 2,
        in_specs=[local] * len(passed),
        out_specs=(far, far),
        scratch_shapes=[
            pltpu.VMEM((rows, width), jnp.bfloat16),
            pltpu.VMEM((chunks, modes, LANES), f32),
            pltpu.SemaphoreType.DMA((2 + (2 if blocks % 4 == 0 else 1),)),
        ],
        compiler_params=pltpu.CompilerParams(vmem_limit_bytes=8 * 2**20),
        name="finish",
    )(*mixed)


def solution(mesh):
    placed = (P(("dp", "node", "chip"), None),) * 6 + (P(),) * 6
    return jax.shard_map(
        shards,
        mesh=mesh,
        in_specs=placed,
        out_specs=(P(("dp", "node", "chip"), None), P(("dp", "node", "chip"), None)),
        check_vma=False,
    )
```

```python
import functools

import jax
import jax.numpy as jnp
from jax import lax
from jax.experimental import pallas as pl
from jax.experimental.pallas import tpu as pltpu
from jax.sharding import PartitionSpec as P

LANES = 128
SUB = 8
LINK = jnp.bfloat16
GROUP = ("node", "chip")


def paired(n, blocks):
    return n % 2 == 0 and blocks % 2 == 0


def far(c, partial, gates, terms, starts, shift, carry, hops, made, full):
    chunks, modes = starts.shape[1], starts.shape[2]
    earlier = carry[c]
    hop = hops[c]
    for a in range(chunks):
        full[a] = starts[c, a] + earlier
        earlier = hop * earlier
        if a == 0:
            earlier = earlier + shift[c]
    cols = pl.ds(pl.multiple_of(c * LANES, LANES), LANES)
    for top in range(0, chunks, SUB):
        span = range(top, min(top + SUB, chunks))
        totals = [partial[c, pl.ds(a * SUB, SUB)] for a in span]
        for m in range(modes):
            term = terms[c, m]
            totals = [total + term * full[a, pl.ds(m, 1)] for a, total in zip(span, totals)]
        first = pl.ds(top * SUB, len(span) * SUB)
        made[first, cols] = (gates[c, first] * jnp.concatenate(totals)).astype(jnp.bfloat16)


def mixer(n, chips, *refs):
    streams, kept = refs[:6], refs[6:12]
    se, made, partial, gates, terms, starts, shift, carry, hops = refs[12:21]
    (
        held, halo, arrived, sent, ext, extended, u_li, near, hold, own, inner, tally, lent, full,
        se_feature, se_filter, li_feature, residue, rate, skip, in_sem, part_sem, fixed_sem, halo_send, halo_recv, pair_send, pair_recv, state_send, state_recv, swap_send, swap_recv, ready_sem,
    ) = refs[21:]
    rows, width = held.shape[1], held.shape[2]
    blocks = width // LANES
    chunks = rows // SUB
    modes = rate.shape[0]
    lags = se_filter.shape[0]
    pair = 2 if paired(n, blocks) else 1
    half = blocks // pair
    dp = lax.axis_index("dp")
    me = lax.axis_index("node") * chips + lax.axis_index("chip")

    def device(index):
        return (dp, lax.div(index, chips), lax.rem(index, chips))

    order = (4, 5, 3, 1, 2, 0)
    parts = part_sem.shape[1]
    each = width // parts
    loads = [pltpu.make_async_copy(streams[i], held.at[i], in_sem.at[i]) for i in range(4)]

    def piece(i, part):
        cols = pl.ds(part * each, each)
        return pltpu.make_async_copy(streams[i].at[:, cols], held.at[i, :, cols], part_sem.at[i - 4, part])

    fixed = (se_feature, se_filter, li_feature, residue, rate, skip)
    fixed_loads = [pltpu.make_async_copy(kept[i], fixed[i], fixed_sem.at[i]) for i in range(6)]
    for i in (4, 2):
        fixed_loads[i].start()
    for part in range(parts):
        for i in (4, 5):
            piece(i, part).start()

    barrier = pltpu.get_barrier_semaphore()

    side = lax.rem(me, pair)
    odd_core = lax.rem(me, 2) == 1

    def hail(semaphore, other):
        pl.semaphore_signal(semaphore, inc=1, device_id=device(other), device_id_type=pl.DeviceIdType.MESH)

    def hail_if(condition, semaphore, other):
        @pl.when(condition)
        def _():
            hail(semaphore, other)

    if pair == 2:
        hail_if(me > 0, barrier, me - 1)
        hail_if(jnp.logical_not(odd_core), barrier, me + 1)
        hail_if(odd_core & (me > 1), barrier, me - 2)
        hail_if(odd_core & (me < n - 1), barrier, me + 2)
    else:
        @pl.loop(0, n)
        def _(other):
            hail_if(other != me, barrier, other)

    def meet():
        if pair == 2:
            pl.semaphore_wait(barrier, jnp.where(odd_core, 1 + 2 * (me < n - 1).astype(jnp.int32) + (me > 1).astype(jnp.int32), 1))
            if n > 4:
                hail_if(me == n - 3, ready_sem, me - 2)
        else:
            pl.semaphore_wait(barrier, n - 1)

    for i in range(6):
        ext[i, pl.ds(0, 2 * SUB)] = jnp.zeros((2 * SUB, LANES), jnp.float32)

    def columns(c):
        return pl.ds(pl.multiple_of(c * LANES, LANES), LANES)

    def featurized(i, c, taps, stream, early):
        cols = columns(c)
        if i not in (4, 5):
            ext[i, pl.ds(SUB, SUB)] = halo[i, :, cols].astype(jnp.float32)
        ext[i, pl.ds(2 * SUB, rows)] = held[i, :, cols].astype(jnp.float32)
        first, count = 2 * SUB - early, rows + early
        total = taps[0, pl.ds(stream, 1), cols] * ext[i, pl.ds(first, count)]
        for lag in (1, 2):
            total = total + taps[lag, pl.ds(stream, 1), cols] * ext[i, pl.ds(first - lag, count)]
        return total

    def local_states(c):
        cols = columns(c)
        product = featurized(4, c, li_feature, 1, 0) * featurized(5, c, li_feature, 2, 0)
        u_li[c, pl.ds(0, SUB)] = jnp.zeros((SUB, LANES), jnp.float32)
        u_li[c, pl.ds(SUB, rows)] = product.astype(jnp.bfloat16).astype(jnp.float32)
        pace = rate[:, cols]
        powers = [None] + [jnp.exp(-pace * float(k)) for k in range(1, SUB + 1)]
        state = jnp.zeros((modes, LANES), jnp.float32)
        for a in range(chunks):
            starts[c, a] = state
            new = jnp.broadcast_to(u_li[c, pl.ds(SUB + a * SUB + SUB - 1, 1)], (modes, LANES))
            for b in range(SUB - 1):
                new = new + powers[SUB - 1 - b] * u_li[c, pl.ds(SUB + a * SUB + b, 1)]
            state = powers[SUB] * state + new
        own[c] = state

    tail = (2, SUB, SUB, 2, 2, 2)

    def halo_copy(i):
        return pltpu.make_async_remote_copy(
            src_ref=streams[i].at[pl.ds(rows - tail[i], tail[i])],
            dst_ref=halo.at[i, pl.ds(SUB - tail[i], tail[i])],
            send_sem=halo_send.at[i],
            recv_sem=halo_recv.at[i],
            device_id=device(lax.rem(me + 1, n)),
            device_id_type=pl.DeviceIdType.MESH,
        )

    per = blocks // parts

    def states(first, last):
        @pl.loop(first, last)
        def _(c):
            local_states(c)

    meet()

    @pl.when(me < n - 1)
    def _():
        for i in order:
            halo_copy(i).start()

    for i in (4, 2):
        fixed_loads[i].wait()
    for part in range(parts):
        for i in (4, 5):
            piece(i, part).wait()
        if part == 0:
            for i in (3, 5, 0, 1):
                fixed_loads[i].start()
            for i in (3, 1, 2, 0):
                loads[i].start()
            states(0, per)
        else:
            states(part * per, (part + 1) * per)

    if pair == 2:
        @pl.when(odd_core & (me > 1) & (me < n - 4))
        def _():
            pl.semaphore_wait(ready_sem, 1)
            hail(ready_sem, me - 2)

    @pl.when(me == 0)
    def _():
        halo[...] = jnp.zeros_like(halo)

    if pair == 2:
        @pl.when(lax.rem(me, 2) == 0)
        def _():
            inner[...] = jnp.zeros_like(inner)


    place = lax.broadcasted_iota(jnp.int32, (SUB, LANES), 0)
    step = place.astype(jnp.float32)

    def ready(i):
        @pl.when(me > 0)
        def _():
            halo_copy(i).wait_recv()

    def state_copy(source, target):
        return pltpu.make_async_remote_copy(
            src_ref=sent.at[pl.ds(lax.rem(target, pair) * half, half)],
            dst_ref=arrived.at[source, pl.ds(lax.rem(target, pair) * half, half)],
            send_sem=state_send.at[target],
            recv_sem=state_recv.at[source],
            device_id=device(target),
            device_id_type=pl.DeviceIdType.MESH,
        )

    def pair_copy():
        return pltpu.make_async_remote_copy(
            src_ref=sent,
            dst_ref=inner,
            send_sem=pair_send.at[0],
            recv_sem=pair_recv.at[0],
            device_id=device(me + 1 - 2 * lax.rem(me, 2)),
            device_id_type=pl.DeviceIdType.MESH,
        )

    ready(4)
    ready(5)

    wide = 4 if blocks % 4 == 0 else 1

    def fixed_up(c, j):
        cols = columns(c)

        def opening(i, stream):
            at = 2 * j + i - 4
            ext[at, pl.ds(SUB, SUB)] = halo[i, :, cols].astype(jnp.float32)
            ext[at, pl.ds(2 * SUB, SUB)] = held[i, pl.ds(0, SUB), cols].astype(jnp.float32)
            total = li_feature[0, pl.ds(stream, 1), cols] * ext[at, pl.ds(2 * SUB, SUB)]
            for lag in (1, 2):
                total = total + li_feature[lag, pl.ds(stream, 1), cols] * ext[at, pl.ds(2 * SUB - lag, SUB)]
            return total

        right = (opening(4, 1) * opening(5, 2)).astype(jnp.bfloat16).astype(jnp.float32)
        extended[pl.ds(j * SUB, SUB)] = right - u_li[c, pl.ds(SUB, SUB)]
        u_li[c, pl.ds(SUB, SUB)] = right
        pace = rate[:, cols]
        moved = jnp.exp(-pace * float(SUB - 1)) * extended[pl.ds(j * SUB, 1)]
        moved = moved + jnp.exp(-pace * float(SUB - 2)) * extended[pl.ds(j * SUB + 1, 1)]
        shift[c] = moved
        state = own[c] + jnp.exp(-pace * float(rows - SUB)) * moved
        own[c] = state
        sent[c] = state.astype(sent.dtype)

    @pl.loop(0, blocks // wide)
    def _(many):
        for j in range(wide):
            fixed_up(many * wide + j, j)

    if pair == 2:
        @pl.when(lax.rem(me, 2) == 0)
        def _():
            pair_copy().start()

    for i in (3, 5, 0, 1):
        fixed_loads[i].wait()

    backward = -step

    def filters(c, j):
        cols = columns(c)
        pace = rate[:, cols]
        twice = 2.0 * pace
        small = twice * (1.0 - twice * (0.5 - twice * (1.0 / 6.0 - twice * (1.0 / 24.0 - twice * (1.0 / 120.0)))))
        gap = jnp.where(twice < 0.03125, small, 1.0 - jnp.exp(-twice))
        rows_of = hold.at[j]
        rows_of[pl.ds(0, modes)] = residue[:, cols] * jnp.sqrt(gap)
        rows_of[pl.ds(modes, modes)] = jnp.exp(-pace)
        hops[c] = jnp.exp(-pace * float(SUB))
        total = jnp.zeros((SUB, LANES), jnp.float32)
        for m in range(modes):
            term = rows_of[pl.ds(m, 1)] * jnp.exp(rate[pl.ds(m, 1), cols] * backward)
            total = total + term
            terms[c, m] = term * rows_of[pl.ds(modes + m, 1)]
        rows_of[pl.ds(2 * modes, SUB)] = total
        for lag in range(SUB):
            tap = rows_of[pl.ds(2 * modes + lag, 1)]
            if lag == 0:
                tap = tap + skip[:, cols]
            near[c, pl.ds(lag, 1)] = tap

    twin = hold.shape[0]

    @pl.loop(0, blocks // twin)
    def _(many):
        for j in range(twin):
            filters(many * twin + j, j)

    if pair == 2:
        @pl.when(lax.rem(me, 2) == 1)
        def _():
            pair_copy().wait_recv()

            @pl.loop(0, blocks // wide)
            def _(many):
                for j in range(wide):
                    c = many * wide + j
                    fall = jnp.exp(-rate[:, columns(c)] * float(rows))
                    sent[c] = (fall * inner[c].astype(jnp.float32) + own[c]).astype(sent.dtype)

    leads = lax.rem(me, pair) == pair - 1
    slot = lax.div(me, pair)

    def send_states(first, last):
        @pl.when(leads)
        def _():
            @pl.loop(first, last)
            def _(target):
                state_copy(slot, target).start()

    if pair == 2:
        send_states(me + 1, jnp.minimum(me + 3, n))

        if n > 4:
            @pl.when(me == 1)
            def _():
                pl.semaphore_wait(ready_sem, 1)

        send_states(me + 3, n)
    else:
        send_states(me + 1, n)

    loads[3].wait()
    ready(3)

    @pl.loop(0, blocks)
    def _(c):
        gates[c] = featurized(3, c, li_feature, 0, 0)
        taps = [near[c, pl.ds(lag, 1)] for lag in range(SUB)]
        for top in range(0, chunks, SUB):
            count = min(SUB, chunks - top)
            tokens = [u_li[c, pl.ds(SUB + top * SUB + b, count, SUB)] for b in range(SUB)]
            for b in range(SUB):
                total = taps[0] * tokens[b]
                for lag in range(1, b + 1):
                    total = total + taps[lag] * tokens[b - lag]
                partial[c, pl.ds(top * SUB + b, count, SUB)] = total

    for i in (1, 2, 0):
        loads[i].wait()
        ready(i)

    @pl.loop(0, blocks)
    def _(c):
        cols = columns(c)
        product = featurized(1, c, se_feature, 1, SUB) * featurized(2, c, se_feature, 2, SUB)
        extended[...] = product.astype(jnp.bfloat16).astype(jnp.float32)
        mixed = se_filter[pl.ds(0, 1), cols] * extended[pl.ds(SUB, rows)]
        for lag in range(1, lags):
            mixed = mixed + se_filter[pl.ds(lag, 1), cols] * extended[pl.ds(SUB - lag, rows)]
        se[:, cols] = (featurized(0, c, se_feature, 0, 0) * mixed).astype(jnp.bfloat16)

    odd = lax.rem(jnp.full((modes, LANES), me, jnp.int32), 2) == 1
    step_by = 4 if half % 4 == 0 else 1

    def by_four(first, body):
        @pl.loop(0, half // step_by)
        def _(many):
            for j in range(step_by):
                body(first + many * step_by + j)

    def cleared(c):
        tally[c] = jnp.zeros((modes, LANES), jnp.float32)

    def summed(source):
        def body(c):
            fall = jnp.exp(-rate[:, columns(c)] * float(rows * pair))
            tally[c] = fall * tally[c] + arrived[source, c].astype(jnp.float32)

        return body

    def lend(c):
        lent[c] = tally[c].astype(lent.dtype)

    def carried_in(c, before):
        if pair == 2:
            within = jnp.exp(-rate[:, columns(c)] * float(rows)) * before + inner[c].astype(jnp.float32)
            before = jnp.where(odd, within, before)
        carry[c] = before

    ours, theirs = side * half, (pair - 1 - side) * half
    by_four(ours, cleared)

    @pl.loop(0, slot)
    def _(source):
        state_copy(source, me).wait_recv()
        by_four(ours, summed(source))

    def swap_copy(first):
        return pltpu.make_async_remote_copy(
            src_ref=lent.at[pl.ds(first, half)],
            dst_ref=lent.at[pl.ds(first, half)],
            send_sem=swap_send.at[0],
            recv_sem=swap_recv.at[0],
            device_id=device(me + 1 - 2 * lax.rem(me, 2)),
            device_id_type=pl.DeviceIdType.MESH,
        )

    if pair == 2:
        @pl.when(slot > 0)
        def _():
            by_four(ours, lend)
            swap_copy(ours).start()

        @pl.when(slot == 0)
        def _():
            lent[...] = jnp.zeros_like(lent)

    by_four(ours, lambda c: carried_in(c, tally[c]))

    @pl.loop(0, half)
    def _(c):
        far(ours + c, partial, gates, terms, starts, shift, carry, hops, made, full)

    if pair == 2:
        @pl.when(slot > 0)
        def _():
            swap_copy(theirs).wait_recv()

        by_four(theirs, lambda c: carried_in(c, lent[c].astype(jnp.float32)))

        @pl.when(slot > 0)
        def _():
            swap_copy(ours).wait_send()

    @pl.when(me < n - 1)
    def _():
        for i in range(6):
            halo_copy(i).wait_send()

    if pair == 2:
        @pl.when(lax.rem(me, 2) == 0)
        def _():
            pair_copy().wait_send()

    @pl.when(leads)
    def _():
        @pl.loop(me + 1, n)
        def _(target):
            state_copy(slot, target).wait_send()


def finish(n, chips, se, made, partial, gates, terms, starts, shift, carry, hops, se_out, li_out, rest, full, sems):
    blocks = partial.shape[0]
    width = se.shape[1]
    pair = 2 if paired(n, blocks) else 1
    half = blocks // pair
    me = lax.axis_index("node") * chips + lax.axis_index("chip")
    ours = lax.rem(me, pair) * half
    theirs = half - ours

    def columns(first, count):
        return pl.ds(pl.multiple_of(first * LANES, LANES), count * LANES)

    own = columns(ours, half)
    done = [pltpu.make_async_copy(se, se_out, sems.at[0]), pltpu.make_async_copy(made.at[:, own], li_out.at[:, own], sems.at[1])]
    for copy in done:
        copy.start()
    if pair == 2:
        parts = sems.shape[0] - 2
        each = half // parts
        for part in range(parts):
            @pl.loop(part * each, (part + 1) * each)
            def _(c):
                far(theirs + c, partial, gates, terms, starts, shift, carry, hops, rest, full)

            cols = columns(theirs + part * each, each)
            done.append(pltpu.make_async_copy(rest.at[:, cols], li_out.at[:, cols], sems.at[2 + part]))
            done[-1].start()
    for copy in done:
        copy.wait()


def shards(*args):
    rows, width = args[0].shape
    modes = args[10].shape[0]
    n, chips = lax.axis_size(GROUP), lax.axis_size("chip")
    blocks, chunks = width // LANES, rows // SUB
    f32 = jnp.float32
    far = pl.BlockSpec(memory_space=pltpu.HBM)
    local = pl.BlockSpec(memory_space=pltpu.VMEM)
    operands = args[:11] + (args[11][None],)
    words = rows * width * 10 + width * modes * (3 * chunks + 3 * SUB + 8 + n)
    budget = min(4 * words + 8 * 2**20, 60 * 2**20)
    parts = 4 if blocks % 4 == 0 else 1
    passed = ((rows, width), jnp.bfloat16), ((rows, width), jnp.bfloat16), *(((blocks, *shape, LANES), f32) for shape in ((rows,), (rows,), (modes, SUB), (chunks, modes), (modes,), (modes,), (modes,)))
    mixed = pl.pallas_call(
        functools.partial(mixer, n, chips),
        out_shape=tuple(jax.ShapeDtypeStruct(*one) for one in passed),
        in_specs=[far] * 12,
        out_specs=(local,) * len(passed),
        scratch_shapes=[
            pltpu.VMEM((6, rows, width), jnp.bfloat16),
            pltpu.VMEM((6, SUB, width), jnp.bfloat16),
            pltpu.VMEM((n, blocks, modes, LANES), LINK),
            pltpu.VMEM((blocks, modes, LANES), LINK),
            pltpu.VMEM((8, rows + 2 * SUB, LANES), f32),
            pltpu.VMEM((rows + SUB, LANES), f32),
            pltpu.VMEM((blocks, rows + SUB, LANES), f32),
            pltpu.VMEM((blocks, SUB, LANES), f32),
            pltpu.VMEM((2 if blocks % 2 == 0 else 1, 2 * modes + SUB, LANES), f32),
            pltpu.VMEM((blocks, modes, LANES), f32),
            pltpu.VMEM((blocks, modes, LANES), LINK),
            pltpu.VMEM((blocks, modes, LANES), f32),
            pltpu.VMEM((blocks, modes, LANES), LINK),
            pltpu.VMEM((chunks, modes, LANES), f32),
            *[pltpu.VMEM(array.shape, f32) for array in operands[6:]],
            pltpu.SemaphoreType.DMA((4,)),
            pltpu.SemaphoreType.DMA((2, parts)),
            pltpu.SemaphoreType.DMA((6,)),
            pltpu.SemaphoreType.DMA((6,)),
            pltpu.SemaphoreType.DMA((6,)),
            pltpu.SemaphoreType.DMA((1,)),
            pltpu.SemaphoreType.DMA((1,)),
            pltpu.SemaphoreType.DMA((n,)),
            pltpu.SemaphoreType.DMA((n,)),
            pltpu.SemaphoreType.DMA((1,)),
            pltpu.SemaphoreType.DMA((1,)),
            pltpu.SemaphoreType.REGULAR,
        ],
        compiler_params=pltpu.CompilerParams(collective_id=0, has_side_effects=True, vmem_limit_bytes=budget),
        name="mixer",
    )(*(pltpu.with_memory_space_constraint(array, pltpu.HBM) for array in operands))
    return pl.pallas_call(
        functools.partial(finish, n, chips),
        out_shape=(jax.ShapeDtypeStruct((rows, width), jnp.bfloat16),) * 2,
        in_specs=[local] * len(passed),
        out_specs=(far, far),
        scratch_shapes=[
            pltpu.VMEM((rows, width), jnp.bfloat16),
            pltpu.VMEM((chunks, modes, LANES), f32),
            pltpu.SemaphoreType.DMA((2 + (2 if blocks % 4 == 0 else 1),)),
        ],
        compiler_params=pltpu.CompilerParams(vmem_limit_bytes=8 * 2**20),
        name="finish",
    )(*mixed)


def solution(mesh):
    placed = (P(("dp", "node", "chip"), None),) * 6 + (P(),) * 6
    return jax.shard_map(
        shards,
        mesh=mesh,
        in_specs=placed,
        out_specs=(P(("dp", "node", "chip"), None), P(("dp", "node", "chip"), None)),
        check_vma=False,
    )
```

```python
import functools

import jax
import jax.numpy as jnp
from jax import lax
from jax.experimental import pallas as pl
from jax.experimental.pallas import tpu as pltpu
from jax.sharding import PartitionSpec as P

LANES = 128
SUB = 8
LINK = jnp.bfloat16
GROUP = ("node", "chip")


def paired(n, blocks):
    return n % 2 == 0 and blocks % 2 == 0


def far(c, partial, gates, terms, starts, shift, carry, hops, made, full):
    chunks, modes = starts.shape[1], starts.shape[2]
    earlier = carry[c]
    hop = hops[c]
    for a in range(chunks):
        full[a] = starts[c, a] + earlier
        earlier = hop * earlier
        if a == 0:
            earlier = earlier + shift[c]
    cols = pl.ds(pl.multiple_of(c * LANES, LANES), LANES)
    for top in range(0, chunks, SUB):
        span = range(top, min(top + SUB, chunks))
        totals = [partial[c, pl.ds(a * SUB, SUB)] for a in span]
        for m in range(modes):
            term = terms[c, m]
            totals = [total + term * full[a, pl.ds(m, 1)] for a, total in zip(span, totals)]
        first = pl.ds(top * SUB, len(span) * SUB)
        made[first, cols] = (gates[c, first] * jnp.concatenate(totals)).astype(jnp.bfloat16)


def mixer(n, chips, *refs):
    streams, kept = refs[:6], refs[6:12]
    se, made, partial, gates, terms, starts, shift, carry, hops = refs[12:21]
    (
        held, halo, arrived, sent, ext, extended, u_li, near, hold, own, inner, tally, lent, full,
        se_feature, se_filter, li_feature, residue, rate, skip, in_sem, part_sem, fixed_sem, halo_send, halo_recv, pair_send, pair_recv, state_send, state_recv, swap_send, swap_recv, ready_sem,
    ) = refs[21:]
    rows, width = held.shape[1], held.shape[2]
    blocks = width // LANES
    chunks = rows // SUB
    modes = rate.shape[0]
    lags = se_filter.shape[0]
    pair = 2 if paired(n, blocks) else 1
    half = blocks // pair
    dp = lax.axis_index("dp")
    me = lax.axis_index("node") * chips + lax.axis_index("chip")

    def device(index):
        return (dp, lax.div(index, chips), lax.rem(index, chips))

    order = (4, 5, 3, 1, 2, 0)
    parts = part_sem.shape[1]
    each = width // parts
    loads = [pltpu.make_async_copy(streams[i], held.at[i], in_sem.at[i]) for i in range(4)]

    def piece(i, part):
        cols = pl.ds(part * each, each)
        return pltpu.make_async_copy(streams[i].at[:, cols], held.at[i, :, cols], part_sem.at[i - 4, part])

    fixed = (se_feature, se_filter, li_feature, residue, rate, skip)
    fixed_loads = [pltpu.make_async_copy(kept[i], fixed[i], fixed_sem.at[i]) for i in range(6)]
    for i in (4, 2):
        fixed_loads[i].start()
    for part in range(parts):
        for i in (4, 5):
            piece(i, part).start()

    barrier = pltpu.get_barrier_semaphore()

    side = lax.rem(me, pair)
    odd_core = lax.rem(me, 2) == 1

    def hail(semaphore, other):
        pl.semaphore_signal(semaphore, inc=1, device_id=device(other), device_id_type=pl.DeviceIdType.MESH)

    def hail_if(condition, semaphore, other):
        @pl.when(condition)
        def _():
            hail(semaphore, other)

    if pair == 2:
        hail_if(me > 0, barrier, me - 1)
        hail_if(jnp.logical_not(odd_core), barrier, me + 1)
        hail_if(odd_core & (me > 1), barrier, me - 2)
        hail_if(odd_core & (me < n - 1), barrier, me + 2)
    else:
        @pl.loop(0, n)
        def _(other):
            hail_if(other != me, barrier, other)

    def meet():
        if pair == 2:
            pl.semaphore_wait(barrier, jnp.where(odd_core, 1 + 2 * (me < n - 1).astype(jnp.int32) + (me > 1).astype(jnp.int32), 1))
            if n > 4:
                hail_if(me == n - 3, ready_sem, me - 2)
        else:
            pl.semaphore_wait(barrier, n - 1)

    for i in range(6):
        ext[i, pl.ds(0, 2 * SUB)] = jnp.zeros((2 * SUB, LANES), jnp.float32)

    def columns(c):
        return pl.ds(pl.multiple_of(c * LANES, LANES), LANES)

    def featurized(i, c, taps, stream, early):
        cols = columns(c)
        if i not in (4, 5):
            ext[i, pl.ds(SUB, SUB)] = halo[i, :, cols].astype(jnp.float32)
        ext[i, pl.ds(2 * SUB, rows)] = held[i, :, cols].astype(jnp.float32)
        first, count = 2 * SUB - early, rows + early
        total = taps[0, pl.ds(stream, 1), cols] * ext[i, pl.ds(first, count)]
        for lag in (1, 2):
            total = total + taps[lag, pl.ds(stream, 1), cols] * ext[i, pl.ds(first - lag, count)]
        return total

    def local_states(c):
        cols = columns(c)
        product = featurized(4, c, li_feature, 1, 0) * featurized(5, c, li_feature, 2, 0)
        u_li[c, pl.ds(0, SUB)] = jnp.zeros((SUB, LANES), jnp.float32)
        u_li[c, pl.ds(SUB, rows)] = product.astype(jnp.bfloat16).astype(jnp.float32)
        pace = rate[:, cols]
        powers = [None] + [jnp.exp(-pace * float(k)) for k in range(1, SUB + 1)]
        state = jnp.zeros((modes, LANES), jnp.float32)
        for a in range(chunks):
            starts[c, a] = state
            new = jnp.broadcast_to(u_li[c, pl.ds(SUB + a * SUB + SUB - 1, 1)], (modes, LANES))
            for b in range(SUB - 1):
                new = new + powers[SUB - 1 - b] * u_li[c, pl.ds(SUB + a * SUB + b, 1)]
            state = powers[SUB] * state + new
        own[c] = state

    tail = (2, SUB, SUB, 2, 2, 2)

    def halo_copy(i):
        return pltpu.make_async_remote_copy(
            src_ref=streams[i].at[pl.ds(rows - tail[i], tail[i])],
            dst_ref=halo.at[i, pl.ds(SUB - tail[i], tail[i])],
            send_sem=halo_send.at[i],
            recv_sem=halo_recv.at[i],
            device_id=device(lax.rem(me + 1, n)),
            device_id_type=pl.DeviceIdType.MESH,
        )

    per = blocks // parts

    def states(first, last):
        @pl.loop(first, last)
        def _(c):
            local_states(c)

    meet()

    @pl.when(me < n - 1)
    def _():
        for i in order:
            halo_copy(i).start()

    for i in (4, 2):
        fixed_loads[i].wait()
    for part in range(parts):
        for i in (4, 5):
            piece(i, part).wait()
        if part == 0:
            for i in (3, 5, 0, 1):
                fixed_loads[i].start()
            for i in (3, 1, 2, 0):
                loads[i].start()
            states(0, per)
        else:
            states(part * per, (part + 1) * per)

    if pair == 2:
        @pl.when(odd_core & (me > 1) & (me < n - 4))
        def _():
            pl.semaphore_wait(ready_sem, 1)
            hail(ready_sem, me - 2)

    @pl.when(me == 0)
    def _():
        halo[...] = jnp.zeros_like(halo)

    if pair == 2:
        @pl.when(lax.rem(me, 2) == 0)
        def _():
            inner[...] = jnp.zeros_like(inner)


    place = lax.broadcasted_iota(jnp.int32, (SUB, LANES), 0)
    step = place.astype(jnp.float32)

    def ready(i):
        @pl.when(me > 0)
        def _():
            halo_copy(i).wait_recv()

    def state_copy(source, target):
        return pltpu.make_async_remote_copy(
            src_ref=sent.at[pl.ds(lax.rem(target, pair) * half, half)],
            dst_ref=arrived.at[source, pl.ds(lax.rem(target, pair) * half, half)],
            send_sem=state_send.at[target],
            recv_sem=state_recv.at[source],
            device_id=device(target),
            device_id_type=pl.DeviceIdType.MESH,
        )

    def pair_copy():
        return pltpu.make_async_remote_copy(
            src_ref=sent,
            dst_ref=inner,
            send_sem=pair_send.at[0],
            recv_sem=pair_recv.at[0],
            device_id=device(me + 1 - 2 * lax.rem(me, 2)),
            device_id_type=pl.DeviceIdType.MESH,
        )

    ready(4)
    ready(5)

    wide = 4 if blocks % 4 == 0 else 1

    def fixed_up(c, j):
        cols = columns(c)

        def opening(i, stream):
            at = 2 * j + i - 4
            ext[at, pl.ds(SUB, SUB)] = halo[i, :, cols].astype(jnp.float32)
            ext[at, pl.ds(2 * SUB, SUB)] = held[i, pl.ds(0, SUB), cols].astype(jnp.float32)
            total = li_feature[0, pl.ds(stream, 1), cols] * ext[at, pl.ds(2 * SUB, SUB)]
            for lag in (1, 2):
                total = total + li_feature[lag, pl.ds(stream, 1), cols] * ext[at, pl.ds(2 * SUB - lag, SUB)]
            return total

        right = (opening(4, 1) * opening(5, 2)).astype(jnp.bfloat16).astype(jnp.float32)
        extended[pl.ds(j * SUB, SUB)] = right - u_li[c, pl.ds(SUB, SUB)]
        u_li[c, pl.ds(SUB, SUB)] = right
        pace = rate[:, cols]
        moved = jnp.exp(-pace * float(SUB - 1)) * extended[pl.ds(j * SUB, 1)]
        moved = moved + jnp.exp(-pace * float(SUB - 2)) * extended[pl.ds(j * SUB + 1, 1)]
        shift[c] = moved
        state = own[c] + jnp.exp(-pace * float(rows - SUB)) * moved
        own[c] = state
        sent[c] = state.astype(sent.dtype)

    @pl.loop(0, blocks // wide)
    def _(many):
        for j in range(wide):
            fixed_up(many * wide + j, j)

    if pair == 2:
        @pl.when(lax.rem(me, 2) == 0)
        def _():
            pair_copy().start()

    for i in (3, 5, 0, 1):
        fixed_loads[i].wait()

    backward = -step

    def filters(c, j):
        cols = columns(c)
        pace = rate[:, cols]
        twice = 2.0 * pace
        small = twice * (1.0 - twice * (0.5 - twice * (1.0 / 6.0 - twice * (1.0 / 24.0 - twice * (1.0 / 120.0)))))
        gap = jnp.where(twice < 0.03125, small, 1.0 - jnp.exp(-twice))
        rows_of = hold.at[j]
        rows_of[pl.ds(0, modes)] = residue[:, cols] * jnp.sqrt(gap)
        rows_of[pl.ds(modes, modes)] = jnp.exp(-pace)
        hops[c] = jnp.exp(-pace * float(SUB))
        total = jnp.zeros((SUB, LANES), jnp.float32)
        for m in range(modes):
            term = rows_of[pl.ds(m, 1)] * jnp.exp(rate[pl.ds(m, 1), cols] * backward)
            total = total + term
            terms[c, m] = term * rows_of[pl.ds(modes + m, 1)]
        rows_of[pl.ds(2 * modes, SUB)] = total
        for lag in range(SUB):
            tap = rows_of[pl.ds(2 * modes + lag, 1)]
            if lag == 0:
                tap = tap + skip[:, cols]
            near[c, pl.ds(lag, 1)] = tap

    twin = hold.shape[0]

    @pl.loop(0, blocks // twin)
    def _(many):
        for j in range(twin):
            filters(many * twin + j, j)

    loads[3].wait()
    ready(3)

    def li_part(c):
        gates[c] = featurized(3, c, li_feature, 0, 0)
        taps = [near[c, pl.ds(lag, 1)] for lag in range(SUB)]
        for top in range(0, chunks, SUB):
            count = min(SUB, chunks - top)
            tokens = [u_li[c, pl.ds(SUB + top * SUB + b, count, SUB)] for b in range(SUB)]
            for b in range(SUB):
                total = taps[0] * tokens[b]
                for lag in range(1, b + 1):
                    total = total + taps[lag] * tokens[b - lag]
                partial[c, pl.ds(top * SUB + b, count, SUB)] = total

    middle = blocks // 2

    @pl.loop(0, middle)
    def _(c):
        li_part(c)

    if pair == 2:
        @pl.when(lax.rem(me, 2) == 1)
        def _():
            pair_copy().wait_recv()

            @pl.loop(0, blocks // wide)
            def _(many):
                for j in range(wide):
                    c = many * wide + j
                    fall = jnp.exp(-rate[:, columns(c)] * float(rows))
                    sent[c] = (fall * inner[c].astype(jnp.float32) + own[c]).astype(sent.dtype)

    leads = lax.rem(me, pair) == pair - 1
    slot = lax.div(me, pair)

    def send_states(first, last):
        @pl.when(leads)
        def _():
            @pl.loop(first, last)
            def _(target):
                state_copy(slot, target).start()

    if pair == 2:
        send_states(me + 1, jnp.where(me == 1, min(4, n), n))
    else:
        send_states(me + 1, n)

    @pl.loop(middle, blocks)
    def _(c):
        li_part(c)

    if pair == 2 and n > 4:
        @pl.when(me == 1)
        def _():
            pl.semaphore_wait(ready_sem, 1)
            send_states(4, n)

    for i in (1, 2, 0):
        loads[i].wait()
        ready(i)

    @pl.loop(0, blocks)
    def _(c):
        cols = columns(c)
        product = featurized(1, c, se_feature, 1, SUB) * featurized(2, c, se_feature, 2, SUB)
        extended[...] = product.astype(jnp.bfloat16).astype(jnp.float32)
        mixed = se_filter[pl.ds(0, 1), cols] * extended[pl.ds(SUB, rows)]
        for lag in range(1, lags):
            mixed = mixed + se_filter[pl.ds(lag, 1), cols] * extended[pl.ds(SUB - lag, rows)]
        se[:, cols] = (featurized(0, c, se_feature, 0, 0) * mixed).astype(jnp.bfloat16)

    odd = lax.rem(jnp.full((modes, LANES), me, jnp.int32), 2) == 1
    step_by = 4 if half % 4 == 0 else 1

    def by_four(first, body):
        @pl.loop(0, half // step_by)
        def _(many):
            for j in range(step_by):
                body(first + many * step_by + j)

    def cleared(c):
        tally[c] = jnp.zeros((modes, LANES), jnp.float32)

    def summed(source):
        def body(c):
            fall = jnp.exp(-rate[:, columns(c)] * float(rows * pair))
            tally[c] = fall * tally[c] + arrived[source, c].astype(jnp.float32)

        return body

    def lend(c):
        lent[c] = tally[c].astype(lent.dtype)

    def carried_in(c, before):
        if pair == 2:
            within = jnp.exp(-rate[:, columns(c)] * float(rows)) * before + inner[c].astype(jnp.float32)
            before = jnp.where(odd, within, before)
        carry[c] = before

    ours, theirs = side * half, (pair - 1 - side) * half
    by_four(ours, cleared)

    @pl.loop(0, slot)
    def _(source):
        state_copy(source, me).wait_recv()
        by_four(ours, summed(source))

    def swap_copy(first):
        return pltpu.make_async_remote_copy(
            src_ref=lent.at[pl.ds(first, half)],
            dst_ref=lent.at[pl.ds(first, half)],
            send_sem=swap_send.at[0],
            recv_sem=swap_recv.at[0],
            device_id=device(me + 1 - 2 * lax.rem(me, 2)),
            device_id_type=pl.DeviceIdType.MESH,
        )

    if pair == 2:
        @pl.when(slot > 0)
        def _():
            by_four(ours, lend)
            swap_copy(ours).start()

        @pl.when(slot == 0)
        def _():
            lent[...] = jnp.zeros_like(lent)

    by_four(ours, lambda c: carried_in(c, tally[c]))

    @pl.loop(0, half)
    def _(c):
        far(ours + c, partial, gates, terms, starts, shift, carry, hops, made, full)

    if pair == 2:
        @pl.when(slot > 0)
        def _():
            swap_copy(theirs).wait_recv()

        by_four(theirs, lambda c: carried_in(c, lent[c].astype(jnp.float32)))

        @pl.when(slot > 0)
        def _():
            swap_copy(ours).wait_send()

    @pl.when(me < n - 1)
    def _():
        for i in range(6):
            halo_copy(i).wait_send()

    if pair == 2:
        @pl.when(lax.rem(me, 2) == 0)
        def _():
            pair_copy().wait_send()

    @pl.when(leads)
    def _():
        @pl.loop(me + 1, n)
        def _(target):
            state_copy(slot, target).wait_send()


def finish(n, chips, se, made, partial, gates, terms, starts, shift, carry, hops, se_out, li_out, rest, full, sems):
    blocks = partial.shape[0]
    width = se.shape[1]
    pair = 2 if paired(n, blocks) else 1
    half = blocks // pair
    me = lax.axis_index("node") * chips + lax.axis_index("chip")
    ours = lax.rem(me, pair) * half
    theirs = half - ours

    def columns(first, count):
        return pl.ds(pl.multiple_of(first * LANES, LANES), count * LANES)

    own = columns(ours, half)
    done = [pltpu.make_async_copy(se, se_out, sems.at[0]), pltpu.make_async_copy(made.at[:, own], li_out.at[:, own], sems.at[1])]
    for copy in done:
        copy.start()
    if pair == 2:
        parts = sems.shape[0] - 2
        each = half // parts
        for part in range(parts):
            @pl.loop(part * each, (part + 1) * each)
            def _(c):
                far(theirs + c, partial, gates, terms, starts, shift, carry, hops, rest, full)

            cols = columns(theirs + part * each, each)
            done.append(pltpu.make_async_copy(rest.at[:, cols], li_out.at[:, cols], sems.at[2 + part]))
            done[-1].start()
    for copy in done:
        copy.wait()


def shards(*args):
    rows, width = args[0].shape
    modes = args[10].shape[0]
    n, chips = lax.axis_size(GROUP), lax.axis_size("chip")
    blocks, chunks = width // LANES, rows // SUB
    f32 = jnp.float32
    far = pl.BlockSpec(memory_space=pltpu.HBM)
    local = pl.BlockSpec(memory_space=pltpu.VMEM)
    operands = args[:11] + (args[11][None],)
    words = rows * width * 10 + width * modes * (3 * chunks + 3 * SUB + 8 + n)
    budget = min(4 * words + 8 * 2**20, 60 * 2**20)
    parts = 4 if blocks % 4 == 0 else 1
    passed = ((rows, width), jnp.bfloat16), ((rows, width), jnp.bfloat16), *(((blocks, *shape, LANES), f32) for shape in ((rows,), (rows,), (modes, SUB), (chunks, modes), (modes,), (modes,), (modes,)))
    mixed = pl.pallas_call(
        functools.partial(mixer, n, chips),
        out_shape=tuple(jax.ShapeDtypeStruct(*one) for one in passed),
        in_specs=[far] * 12,
        out_specs=(local,) * len(passed),
        scratch_shapes=[
            pltpu.VMEM((6, rows, width), jnp.bfloat16),
            pltpu.VMEM((6, SUB, width), jnp.bfloat16),
            pltpu.VMEM((n, blocks, modes, LANES), LINK),
            pltpu.VMEM((blocks, modes, LANES), LINK),
            pltpu.VMEM((8, rows + 2 * SUB, LANES), f32),
            pltpu.VMEM((rows + SUB, LANES), f32),
            pltpu.VMEM((blocks, rows + SUB, LANES), f32),
            pltpu.VMEM((blocks, SUB, LANES), f32),
            pltpu.VMEM((2 if blocks % 2 == 0 else 1, 2 * modes + SUB, LANES), f32),
            pltpu.VMEM((blocks, modes, LANES), f32),
            pltpu.VMEM((blocks, modes, LANES), LINK),
            pltpu.VMEM((blocks, modes, LANES), f32),
            pltpu.VMEM((blocks, modes, LANES), LINK),
            pltpu.VMEM((chunks, modes, LANES), f32),
            *[pltpu.VMEM(array.shape, f32) for array in operands[6:]],
            pltpu.SemaphoreType.DMA((4,)),
            pltpu.SemaphoreType.DMA((2, parts)),
            pltpu.SemaphoreType.DMA((6,)),
            pltpu.SemaphoreType.DMA((6,)),
            pltpu.SemaphoreType.DMA((6,)),
            pltpu.SemaphoreType.DMA((1,)),
            pltpu.SemaphoreType.DMA((1,)),
            pltpu.SemaphoreType.DMA((n,)),
            pltpu.SemaphoreType.DMA((n,)),
            pltpu.SemaphoreType.DMA((1,)),
            pltpu.SemaphoreType.DMA((1,)),
            pltpu.SemaphoreType.REGULAR,
        ],
        compiler_params=pltpu.CompilerParams(collective_id=0, has_side_effects=True, vmem_limit_bytes=budget),
        name="mixer",
    )(*(pltpu.with_memory_space_constraint(array, pltpu.HBM) for array in operands))
    return pl.pallas_call(
        functools.partial(finish, n, chips),
        out_shape=(jax.ShapeDtypeStruct((rows, width), jnp.bfloat16),) * 2,
        in_specs=[local] * len(passed),
        out_specs=(far, far),
        scratch_shapes=[
            pltpu.VMEM((rows, width), jnp.bfloat16),
            pltpu.VMEM((chunks, modes, LANES), f32),
            pltpu.SemaphoreType.DMA((2 + (2 if blocks % 4 == 0 else 1),)),
        ],
        compiler_params=pltpu.CompilerParams(vmem_limit_bytes=8 * 2**20),
        name="finish",
    )(*mixed)


def solution(mesh):
    placed = (P(("dp", "node", "chip"), None),) * 6 + (P(),) * 6
    return jax.shard_map(
        shards,
        mesh=mesh,
        in_specs=placed,
        out_specs=(P(("dp", "node", "chip"), None), P(("dp", "node", "chip"), None)),
        check_vma=False,
    )
```

```python
import functools

import jax
import jax.numpy as jnp
from jax import lax
from jax.experimental import pallas as pl
from jax.experimental.pallas import tpu as pltpu
from jax.sharding import PartitionSpec as P

LANES = 128
SUB = 8
LINK = jnp.bfloat16
GROUP = ("node", "chip")


def paired(n, blocks):
    return n % 2 == 0 and blocks % 2 == 0


def far(c, partial, gates, terms, starts, shift, carry, hops, made, full):
    chunks, modes = starts.shape[1], starts.shape[2]
    earlier = carry[c]
    hop = hops[c]
    for a in range(chunks):
        full[a] = starts[c, a] + earlier
        earlier = hop * earlier
        if a == 0:
            earlier = earlier + shift[c]
    cols = pl.ds(pl.multiple_of(c * LANES, LANES), LANES)
    for top in range(0, chunks, SUB):
        span = range(top, min(top + SUB, chunks))
        totals = [partial[c, pl.ds(a * SUB, SUB)] for a in span]
        for m in range(modes):
            term = terms[c, m]
            totals = [total + term * full[a, pl.ds(m, 1)] for a, total in zip(span, totals)]
        first = pl.ds(top * SUB, len(span) * SUB)
        made[first, cols] = (gates[c, first] * jnp.concatenate(totals)).astype(jnp.bfloat16)


def mixer(n, chips, *refs):
    streams, kept = refs[:6], refs[6:12]
    se, made, partial, gates, terms, starts, shift, carry, hops = refs[12:21]
    (
        held, halo, arrived, sent, ext, extended, u_li, near, hold, own, inner, tally, lent, full,
        se_feature, se_filter, li_feature, residue, rate, skip, in_sem, part_sem, fixed_sem, halo_send, halo_recv, pair_send, pair_recv, state_send, state_recv, swap_send, swap_recv, ready_sem,
    ) = refs[21:]
    rows, width = held.shape[1], held.shape[2]
    blocks = width // LANES
    chunks = rows // SUB
    modes = rate.shape[0]
    lags = se_filter.shape[0]
    pair = 2 if paired(n, blocks) else 1
    half = blocks // pair
    dp = lax.axis_index("dp")
    me = lax.axis_index("node") * chips + lax.axis_index("chip")

    def device(index):
        return (dp, lax.div(index, chips), lax.rem(index, chips))

    order = (4, 5, 3, 1, 2, 0)
    parts = part_sem.shape[1]
    each = width // parts
    loads = [pltpu.make_async_copy(streams[i], held.at[i], in_sem.at[i]) for i in range(4)]

    def piece(i, part):
        cols = pl.ds(part * each, each)
        return pltpu.make_async_copy(streams[i].at[:, cols], held.at[i, :, cols], part_sem.at[i - 4, part])

    fixed = (se_feature, se_filter, li_feature, residue, rate, skip)
    fixed_loads = [pltpu.make_async_copy(kept[i], fixed[i], fixed_sem.at[i]) for i in range(6)]
    for i in (4, 2):
        fixed_loads[i].start()
    for part in range(parts):
        for i in (4, 5):
            piece(i, part).start()

    barrier = pltpu.get_barrier_semaphore()

    side = lax.rem(me, pair)
    odd_core = lax.rem(me, 2) == 1

    def hail(semaphore, other):
        pl.semaphore_signal(semaphore, inc=1, device_id=device(other), device_id_type=pl.DeviceIdType.MESH)

    def hail_if(condition, semaphore, other):
        @pl.when(condition)
        def _():
            hail(semaphore, other)

    if pair == 2:
        hail_if(me > 0, barrier, me - 1)
        hail_if(jnp.logical_not(odd_core), barrier, me + 1)
        hail_if(odd_core & (me > 1), barrier, me - 2)
        hail_if(odd_core & (me < n - 1), barrier, me + 2)
    else:
        @pl.loop(0, n)
        def _(other):
            hail_if(other != me, barrier, other)

    def meet():
        if pair == 2:
            pl.semaphore_wait(barrier, jnp.where(odd_core, 1 + 2 * (me < n - 1).astype(jnp.int32) + (me > 1).astype(jnp.int32), 1))
            if n > 4:
                hail_if(me == n - 3, ready_sem, me - 2)
        else:
            pl.semaphore_wait(barrier, n - 1)

    for i in range(6):
        ext[i, pl.ds(0, 2 * SUB)] = jnp.zeros((2 * SUB, LANES), jnp.float32)

    def columns(c):
        return pl.ds(pl.multiple_of(c * LANES, LANES), LANES)

    def featurized(i, c, taps, stream, early):
        cols = columns(c)
        if i not in (4, 5):
            ext[i, pl.ds(SUB, SUB)] = halo[i, :, cols].astype(jnp.float32)
        ext[i, pl.ds(2 * SUB, rows)] = held[i, :, cols].astype(jnp.float32)
        first, count = 2 * SUB - early, rows + early
        total = taps[0, pl.ds(stream, 1), cols] * ext[i, pl.ds(first, count)]
        for lag in (1, 2):
            total = total + taps[lag, pl.ds(stream, 1), cols] * ext[i, pl.ds(first - lag, count)]
        return total

    def local_states(c):
        cols = columns(c)
        product = featurized(4, c, li_feature, 1, 0) * featurized(5, c, li_feature, 2, 0)
        u_li[c, pl.ds(0, SUB)] = jnp.zeros((SUB, LANES), jnp.float32)
        u_li[c, pl.ds(SUB, rows)] = product.astype(jnp.bfloat16).astype(jnp.float32)
        pace = rate[:, cols]
        powers = [None] + [jnp.exp(-pace * float(k)) for k in range(1, SUB + 1)]
        state = jnp.zeros((modes, LANES), jnp.float32)
        for a in range(chunks):
            starts[c, a] = state
            new = jnp.broadcast_to(u_li[c, pl.ds(SUB + a * SUB + SUB - 1, 1)], (modes, LANES))
            for b in range(SUB - 1):
                new = new + powers[SUB - 1 - b] * u_li[c, pl.ds(SUB + a * SUB + b, 1)]
            state = powers[SUB] * state + new
        own[c] = state

    tail = (2, SUB, SUB, 2, 2, 2)

    def halo_copy(i):
        return pltpu.make_async_remote_copy(
            src_ref=streams[i].at[pl.ds(rows - tail[i], tail[i])],
            dst_ref=halo.at[i, pl.ds(SUB - tail[i], tail[i])],
            send_sem=halo_send.at[i],
            recv_sem=halo_recv.at[i],
            device_id=device(lax.rem(me + 1, n)),
            device_id_type=pl.DeviceIdType.MESH,
        )

    per = blocks // parts

    def states(first, last):
        @pl.loop(first, last)
        def _(c):
            local_states(c)

    for i in (4, 2):
        fixed_loads[i].wait()
    for part in range(parts):
        for i in (4, 5):
            piece(i, part).wait()
        if part == 0:
            for i in (3, 5, 0, 1):
                fixed_loads[i].start()
            for i in (3, 1, 2, 0):
                loads[i].start()
            states(0, per)
            meet()

            @pl.when(me < n - 1)
            def _():
                for i in order:
                    halo_copy(i).start()
        else:
            states(part * per, (part + 1) * per)

    if pair == 2:
        @pl.when(odd_core & (me > 1) & (me < n - 4))
        def _():
            pl.semaphore_wait(ready_sem, 1)
            hail(ready_sem, me - 2)

    @pl.when(me == 0)
    def _():
        halo[...] = jnp.zeros_like(halo)

    if pair == 2:
        @pl.when(lax.rem(me, 2) == 0)
        def _():
            inner[...] = jnp.zeros_like(inner)

    place = lax.broadcasted_iota(jnp.int32, (SUB, LANES), 0)
    step = place.astype(jnp.float32)

    def ready(i):
        @pl.when(me > 0)
        def _():
            halo_copy(i).wait_recv()

    def state_copy(source, target):
        return pltpu.make_async_remote_copy(
            src_ref=sent.at[pl.ds(lax.rem(target, pair) * half, half)],
            dst_ref=arrived.at[source, pl.ds(lax.rem(target, pair) * half, half)],
            send_sem=state_send.at[target],
            recv_sem=state_recv.at[source],
            device_id=device(target),
            device_id_type=pl.DeviceIdType.MESH,
        )

    def pair_copy():
        return pltpu.make_async_remote_copy(
            src_ref=sent,
            dst_ref=inner,
            send_sem=pair_send.at[0],
            recv_sem=pair_recv.at[0],
            device_id=device(me + 1 - 2 * lax.rem(me, 2)),
            device_id_type=pl.DeviceIdType.MESH,
        )

    for i in (3, 5, 0, 1):
        fixed_loads[i].wait()

    backward = -step

    def filters(c, j):
        cols = columns(c)
        pace = rate[:, cols]
        twice = 2.0 * pace
        small = twice * (1.0 - twice * (0.5 - twice * (1.0 / 6.0 - twice * (1.0 / 24.0 - twice * (1.0 / 120.0)))))
        gap = jnp.where(twice < 0.03125, small, 1.0 - jnp.exp(-twice))
        rows_of = hold.at[j]
        rows_of[pl.ds(0, modes)] = residue[:, cols] * jnp.sqrt(gap)
        rows_of[pl.ds(modes, modes)] = jnp.exp(-pace)
        hops[c] = jnp.exp(-pace * float(SUB))
        total = jnp.zeros((SUB, LANES), jnp.float32)
        for m in range(modes):
            term = rows_of[pl.ds(m, 1)] * jnp.exp(rate[pl.ds(m, 1), cols] * backward)
            total = total + term
            terms[c, m] = term * rows_of[pl.ds(modes + m, 1)]
        rows_of[pl.ds(2 * modes, SUB)] = total
        for lag in range(SUB):
            tap = rows_of[pl.ds(2 * modes + lag, 1)]
            if lag == 0:
                tap = tap + skip[:, cols]
            near[c, pl.ds(lag, 1)] = tap

    twin = hold.shape[0]

    early = (lax.rem(me, chips) < pair) & (me >= pair)

    @pl.when(early)
    def _():
        @pl.loop(0, blocks // twin)
        def _(many):
            for j in range(twin):
                filters(many * twin + j, j)

    ready(4)
    ready(5)

    wide = 4 if blocks % 4 == 0 else 1

    def fixed_up(c, j):
        cols = columns(c)

        def opening(i, stream):
            at = 2 * j + i - 4
            ext[at, pl.ds(SUB, SUB)] = halo[i, :, cols].astype(jnp.float32)
            ext[at, pl.ds(2 * SUB, SUB)] = held[i, pl.ds(0, SUB), cols].astype(jnp.float32)
            total = li_feature[0, pl.ds(stream, 1), cols] * ext[at, pl.ds(2 * SUB, SUB)]
            for lag in (1, 2):
                total = total + li_feature[lag, pl.ds(stream, 1), cols] * ext[at, pl.ds(2 * SUB - lag, SUB)]
            return total

        right = (opening(4, 1) * opening(5, 2)).astype(jnp.bfloat16).astype(jnp.float32)
        extended[pl.ds(j * SUB, SUB)] = right - u_li[c, pl.ds(SUB, SUB)]
        u_li[c, pl.ds(SUB, SUB)] = right
        pace = rate[:, cols]
        moved = jnp.exp(-pace * float(SUB - 1)) * extended[pl.ds(j * SUB, 1)]
        moved = moved + jnp.exp(-pace * float(SUB - 2)) * extended[pl.ds(j * SUB + 1, 1)]
        shift[c] = moved
        state = own[c] + jnp.exp(-pace * float(rows - SUB)) * moved
        own[c] = state
        sent[c] = state.astype(sent.dtype)

    @pl.loop(0, blocks // wide)
    def _(many):
        for j in range(wide):
            fixed_up(many * wide + j, j)

    if pair == 2:
        @pl.when(lax.rem(me, 2) == 0)
        def _():
            pair_copy().start()

    @pl.when(jnp.logical_not(early))
    def _():
        @pl.loop(0, blocks // twin)
        def _(many):
            for j in range(twin):
                filters(many * twin + j, j)

    loads[3].wait()
    ready(3)

    def li_part(c):
        gates[c] = featurized(3, c, li_feature, 0, 0)
        taps = [near[c, pl.ds(lag, 1)] for lag in range(SUB)]
        for top in range(0, chunks, SUB):
            count = min(SUB, chunks - top)
            tokens = [u_li[c, pl.ds(SUB + top * SUB + b, count, SUB)] for b in range(SUB)]
            for b in range(SUB):
                total = taps[0] * tokens[b]
                for lag in range(1, b + 1):
                    total = total + taps[lag] * tokens[b - lag]
                partial[c, pl.ds(top * SUB + b, count, SUB)] = total

    middle = blocks // 2

    @pl.loop(0, middle)
    def _(c):
        li_part(c)

    if pair == 2:
        @pl.when(lax.rem(me, 2) == 1)
        def _():
            pair_copy().wait_recv()

            @pl.loop(0, blocks // wide)
            def _(many):
                for j in range(wide):
                    c = many * wide + j
                    fall = jnp.exp(-rate[:, columns(c)] * float(rows))
                    sent[c] = (fall * inner[c].astype(jnp.float32) + own[c]).astype(sent.dtype)

    leads = lax.rem(me, pair) == pair - 1
    slot = lax.div(me, pair)

    def send_states(first, last):
        @pl.when(leads)
        def _():
            @pl.loop(first, last)
            def _(target):
                state_copy(slot, target).start()

    if pair == 2:
        send_states(me + 1, jnp.where(me == 1, min(4, n), n))
    else:
        send_states(me + 1, n)

    @pl.loop(middle, blocks)
    def _(c):
        li_part(c)

    if pair == 2 and n > 4:
        @pl.when(me == 1)
        def _():
            pl.semaphore_wait(ready_sem, 1)
            send_states(4, n)

    for i in (1, 2, 0):
        loads[i].wait()
        ready(i)

    @pl.loop(0, blocks)
    def _(c):
        cols = columns(c)
        product = featurized(1, c, se_feature, 1, SUB) * featurized(2, c, se_feature, 2, SUB)
        extended[...] = product.astype(jnp.bfloat16).astype(jnp.float32)
        mixed = se_filter[pl.ds(0, 1), cols] * extended[pl.ds(SUB, rows)]
        for lag in range(1, lags):
            mixed = mixed + se_filter[pl.ds(lag, 1), cols] * extended[pl.ds(SUB - lag, rows)]
        se[:, cols] = (featurized(0, c, se_feature, 0, 0) * mixed).astype(jnp.bfloat16)

    odd = lax.rem(jnp.full((modes, LANES), me, jnp.int32), 2) == 1
    step_by = 4 if half % 4 == 0 else 1

    def by_four(first, body):
        @pl.loop(0, half // step_by)
        def _(many):
            for j in range(step_by):
                body(first + many * step_by + j)

    def cleared(c):
        tally[c] = jnp.zeros((modes, LANES), jnp.float32)

    def summed(source):
        def body(c):
            fall = jnp.exp(-rate[:, columns(c)] * float(rows * pair))
            tally[c] = fall * tally[c] + arrived[source, c].astype(jnp.float32)

        return body

    def lend(c):
        lent[c] = tally[c].astype(lent.dtype)

    def carried_in(c, before):
        if pair == 2:
            within = jnp.exp(-rate[:, columns(c)] * float(rows)) * before + inner[c].astype(jnp.float32)
            before = jnp.where(odd, within, before)
        carry[c] = before

    ours, theirs = side * half, (pair - 1 - side) * half
    by_four(ours, cleared)

    @pl.loop(0, slot)
    def _(source):
        state_copy(source, me).wait_recv()
        by_four(ours, summed(source))

    def swap_copy(first):
        return pltpu.make_async_remote_copy(
            src_ref=lent.at[pl.ds(first, half)],
            dst_ref=lent.at[pl.ds(first, half)],
            send_sem=swap_send.at[0],
            recv_sem=swap_recv.at[0],
            device_id=device(me + 1 - 2 * lax.rem(me, 2)),
            device_id_type=pl.DeviceIdType.MESH,
        )

    if pair == 2:
        @pl.when(slot > 0)
        def _():
            by_four(ours, lend)
            swap_copy(ours).start()

        @pl.when(slot == 0)
        def _():
            lent[...] = jnp.zeros_like(lent)

    by_four(ours, lambda c: carried_in(c, tally[c]))

    @pl.loop(0, half)
    def _(c):
        far(ours + c, partial, gates, terms, starts, shift, carry, hops, made, full)

    if pair == 2:
        @pl.when(slot > 0)
        def _():
            swap_copy(theirs).wait_recv()

        by_four(theirs, lambda c: carried_in(c, lent[c].astype(jnp.float32)))

        @pl.when(slot > 0)
        def _():
            swap_copy(ours).wait_send()

    @pl.when(me < n - 1)
    def _():
        for i in range(6):
            halo_copy(i).wait_send()

    if pair == 2:
        @pl.when(lax.rem(me, 2) == 0)
        def _():
            pair_copy().wait_send()

    @pl.when(leads)
    def _():
        @pl.loop(me + 1, n)
        def _(target):
            state_copy(slot, target).wait_send()


def finish(n, chips, se, made, partial, gates, terms, starts, shift, carry, hops, se_out, li_out, rest, full, sems):
    blocks = partial.shape[0]
    width = se.shape[1]
    pair = 2 if paired(n, blocks) else 1
    half = blocks // pair
    me = lax.axis_index("node") * chips + lax.axis_index("chip")
    ours = lax.rem(me, pair) * half
    theirs = half - ours

    def columns(first, count):
        return pl.ds(pl.multiple_of(first * LANES, LANES), count * LANES)

    own = columns(ours, half)
    done = [pltpu.make_async_copy(se, se_out, sems.at[0]), pltpu.make_async_copy(made.at[:, own], li_out.at[:, own], sems.at[1])]
    for copy in done:
        copy.start()
    if pair == 2:
        parts = sems.shape[0] - 2
        each = half // parts
        for part in range(parts):
            @pl.loop(part * each, (part + 1) * each)
            def _(c):
                far(theirs + c, partial, gates, terms, starts, shift, carry, hops, rest, full)

            cols = columns(theirs + part * each, each)
            done.append(pltpu.make_async_copy(rest.at[:, cols], li_out.at[:, cols], sems.at[2 + part]))
            done[-1].start()
    for copy in done:
        copy.wait()


def shards(*args):
    rows, width = args[0].shape
    modes = args[10].shape[0]
    n, chips = lax.axis_size(GROUP), lax.axis_size("chip")
    blocks, chunks = width // LANES, rows // SUB
    f32 = jnp.float32
    far = pl.BlockSpec(memory_space=pltpu.HBM)
    local = pl.BlockSpec(memory_space=pltpu.VMEM)
    operands = args[:11] + (args[11][None],)
    words = rows * width * 10 + width * modes * (3 * chunks + 3 * SUB + 8 + n)
    budget = min(4 * words + 8 * 2**20, 60 * 2**20)
    parts = 4 if blocks % 4 == 0 else 1
    passed = ((rows, width), jnp.bfloat16), ((rows, width), jnp.bfloat16), *(((blocks, *shape, LANES), f32) for shape in ((rows,), (rows,), (modes, SUB), (chunks, modes), (modes,), (modes,), (modes,)))
    mixed = pl.pallas_call(
        functools.partial(mixer, n, chips),
        out_shape=tuple(jax.ShapeDtypeStruct(*one) for one in passed),
        in_specs=[far] * 12,
        out_specs=(local,) * len(passed),
        scratch_shapes=[
            pltpu.VMEM((6, rows, width), jnp.bfloat16),
            pltpu.VMEM((6, SUB, width), jnp.bfloat16),
            pltpu.VMEM((n, blocks, modes, LANES), LINK),
            pltpu.VMEM((blocks, modes, LANES), LINK),
            pltpu.VMEM((8, rows + 2 * SUB, LANES), f32),
            pltpu.VMEM((rows + SUB, LANES), f32),
            pltpu.VMEM((blocks, rows + SUB, LANES), f32),
            pltpu.VMEM((blocks, SUB, LANES), f32),
            pltpu.VMEM((2 if blocks % 2 == 0 else 1, 2 * modes + SUB, LANES), f32),
            pltpu.VMEM((blocks, modes, LANES), f32),
            pltpu.VMEM((blocks, modes, LANES), LINK),
            pltpu.VMEM((blocks, modes, LANES), f32),
            pltpu.VMEM((blocks, modes, LANES), LINK),
            pltpu.VMEM((chunks, modes, LANES), f32),
            *[pltpu.VMEM(array.shape, f32) for array in operands[6:]],
            pltpu.SemaphoreType.DMA((4,)),
            pltpu.SemaphoreType.DMA((2, parts)),
            pltpu.SemaphoreType.DMA((6,)),
            pltpu.SemaphoreType.DMA((6,)),
            pltpu.SemaphoreType.DMA((6,)),
            pltpu.SemaphoreType.DMA((1,)),
            pltpu.SemaphoreType.DMA((1,)),
            pltpu.SemaphoreType.DMA((n,)),
            pltpu.SemaphoreType.DMA((n,)),
            pltpu.SemaphoreType.DMA((1,)),
            pltpu.SemaphoreType.DMA((1,)),
            pltpu.SemaphoreType.REGULAR,
        ],
        compiler_params=pltpu.CompilerParams(collective_id=0, has_side_effects=True, vmem_limit_bytes=budget),
        name="mixer",
    )(*(pltpu.with_memory_space_constraint(array, pltpu.HBM) for array in operands))
    return pl.pallas_call(
        functools.partial(finish, n, chips),
        out_shape=(jax.ShapeDtypeStruct((rows, width), jnp.bfloat16),) * 2,
        in_specs=[local] * len(passed),
        out_specs=(far, far),
        scratch_shapes=[
            pltpu.VMEM((rows, width), jnp.bfloat16),
            pltpu.VMEM((chunks, modes, LANES), f32),
            pltpu.SemaphoreType.DMA((2 + (2 if blocks % 4 == 0 else 1),)),
        ],
        compiler_params=pltpu.CompilerParams(vmem_limit_bytes=8 * 2**20),
        name="finish",
    )(*mixed)


def solution(mesh):
    placed = (P(("dp", "node", "chip"), None),) * 6 + (P(),) * 6
    return jax.shard_map(
        shards,
        mesh=mesh,
        in_specs=placed,
        out_specs=(P(("dp", "node", "chip"), None), P(("dp", "node", "chip"), None)),
        check_vma=False,
    )
```

```python
import functools

import jax
import jax.numpy as jnp
from jax import lax
from jax.experimental import pallas as pl
from jax.experimental.pallas import tpu as pltpu
from jax.sharding import PartitionSpec as P

LANES = 128
SUB = 8
LINK = jnp.bfloat16
GROUP = ("node", "chip")


def paired(n, blocks):
    return n % 2 == 0 and blocks % 2 == 0


def far(c, partial, gates, terms, starts, shift, carry, hops, made, full):
    chunks, modes = starts.shape[1], starts.shape[2]
    earlier = carry[c]
    hop = hops[c]
    for a in range(chunks):
        full[a] = starts[c, a] + earlier
        earlier = hop * earlier
        if a == 0:
            earlier = earlier + shift[c]
    cols = pl.ds(pl.multiple_of(c * LANES, LANES), LANES)
    for top in range(0, chunks, SUB):
        span = range(top, min(top + SUB, chunks))
        totals = [partial[c, pl.ds(a * SUB, SUB)] for a in span]
        for m in range(modes):
            term = terms[c, m]
            totals = [total + term * full[a, pl.ds(m, 1)] for a, total in zip(span, totals)]
        first = pl.ds(top * SUB, len(span) * SUB)
        made[first, cols] = (gates[c, first] * jnp.concatenate(totals)).astype(jnp.bfloat16)


def mixer(n, chips, *refs):
    streams, kept = refs[:6], refs[6:12]
    se, made, partial, gates, terms, starts, shift, carry, hops = refs[12:21]
    (
        held, halo, arrived, sent, ext, extended, u_li, near, hold, own, inner, tally, lent, full,
        se_feature, se_filter, li_feature, residue, rate, skip, in_sem, part_sem, fixed_sem, halo_send, halo_recv, pair_send, pair_recv, state_send, state_recv, swap_send, swap_recv, ready_sem,
    ) = refs[21:]
    rows, width = held.shape[1], held.shape[2]
    blocks = width // LANES
    chunks = rows // SUB
    modes = rate.shape[0]
    lags = se_filter.shape[0]
    pair = 2 if paired(n, blocks) else 1
    half = blocks // pair
    dp = lax.axis_index("dp")
    me = lax.axis_index("node") * chips + lax.axis_index("chip")

    def device(index):
        return (dp, lax.div(index, chips), lax.rem(index, chips))

    order = (4, 5, 3, 1, 2, 0)
    parts = part_sem.shape[1]
    each = width // parts
    loads = [pltpu.make_async_copy(streams[i], held.at[i], in_sem.at[i]) for i in range(4)]

    def piece(i, part):
        cols = pl.ds(part * each, each)
        return pltpu.make_async_copy(streams[i].at[:, cols], held.at[i, :, cols], part_sem.at[i - 4, part])

    fixed = (se_feature, se_filter, li_feature, residue, rate, skip)
    fixed_loads = [pltpu.make_async_copy(kept[i], fixed[i], fixed_sem.at[i]) for i in range(6)]
    for i in (4, 2):
        fixed_loads[i].start()
    for part in range(parts):
        for i in (4, 5):
            piece(i, part).start()

    barrier = pltpu.get_barrier_semaphore()

    side = lax.rem(me, pair)
    odd_core = lax.rem(me, 2) == 1

    def hail(semaphore, other):
        pl.semaphore_signal(semaphore, inc=1, device_id=device(other), device_id_type=pl.DeviceIdType.MESH)

    def hail_if(condition, semaphore, other):
        @pl.when(condition)
        def _():
            hail(semaphore, other)

    if pair == 2:
        hail_if(me > 0, barrier, me - 1)
        hail_if(jnp.logical_not(odd_core), barrier, me + 1)
        hail_if(odd_core & (me > 1), barrier, me - 2)
        hail_if(odd_core & (me < n - 1), barrier, me + 2)
    else:
        @pl.loop(0, n)
        def _(other):
            hail_if(other != me, barrier, other)

    def meet():
        if pair == 2:
            pl.semaphore_wait(barrier, jnp.where(odd_core, 1 + 2 * (me < n - 1).astype(jnp.int32) + (me > 1).astype(jnp.int32), 1))
            if n > 4:
                hail_if(me == n - 3, ready_sem, me - 2)
        else:
            pl.semaphore_wait(barrier, n - 1)

    for i in range(6):
        ext[i, pl.ds(0, 2 * SUB)] = jnp.zeros((2 * SUB, LANES), jnp.float32)

    def columns(c):
        return pl.ds(pl.multiple_of(c * LANES, LANES), LANES)

    def featurized(i, c, taps, stream, early):
        cols = columns(c)
        if i not in (4, 5):
            ext[i, pl.ds(SUB, SUB)] = halo[i, :, cols].astype(jnp.float32)
        ext[i, pl.ds(2 * SUB, rows)] = held[i, :, cols].astype(jnp.float32)
        first, count = 2 * SUB - early, rows + early
        total = taps[0, pl.ds(stream, 1), cols] * ext[i, pl.ds(first, count)]
        for lag in (1, 2):
            total = total + taps[lag, pl.ds(stream, 1), cols] * ext[i, pl.ds(first - lag, count)]
        return total

    def local_states(c):
        cols = columns(c)
        product = featurized(4, c, li_feature, 1, 0) * featurized(5, c, li_feature, 2, 0)
        u_li[c, pl.ds(0, SUB)] = jnp.zeros((SUB, LANES), jnp.float32)
        u_li[c, pl.ds(SUB, rows)] = product.astype(jnp.bfloat16).astype(jnp.float32)
        pace = rate[:, cols]
        powers = [None] + [jnp.exp(-pace * float(k)) for k in range(1, SUB + 1)]
        state = jnp.zeros((modes, LANES), jnp.float32)
        for a in range(chunks):
            starts[c, a] = state
            new = jnp.broadcast_to(u_li[c, pl.ds(SUB + a * SUB + SUB - 1, 1)], (modes, LANES))
            for b in range(SUB - 1):
                new = new + powers[SUB - 1 - b] * u_li[c, pl.ds(SUB + a * SUB + b, 1)]
            state = powers[SUB] * state + new
        own[c] = state

    tail = (2, SUB, SUB, 2, 2, 2)

    def halo_copy(i):
        return pltpu.make_async_remote_copy(
            src_ref=streams[i].at[pl.ds(rows - tail[i], tail[i])],
            dst_ref=halo.at[i, pl.ds(SUB - tail[i], tail[i])],
            send_sem=halo_send.at[i],
            recv_sem=halo_recv.at[i],
            device_id=device(lax.rem(me + 1, n)),
            device_id_type=pl.DeviceIdType.MESH,
        )

    per = blocks // parts

    def states(first, last):
        @pl.loop(first, last)
        def _(c):
            local_states(c)

    for i in (4, 2):
        fixed_loads[i].wait()
    for part in range(parts):
        for i in (4, 5):
            piece(i, part).wait()
        if part == 0:
            for i in (3, 5, 0, 1):
                fixed_loads[i].start()
            for i in (3, 1, 2, 0):
                loads[i].start()
            states(0, per)
            meet()

            @pl.when(me < n - 1)
            def _():
                for i in order:
                    halo_copy(i).start()
        else:
            states(part * per, (part + 1) * per)

    if pair == 2:
        @pl.when(odd_core & (me > 1) & (me < n - 4))
        def _():
            pl.semaphore_wait(ready_sem, 1)
            hail(ready_sem, me - 2)

    @pl.when(me == 0)
    def _():
        halo[...] = jnp.zeros_like(halo)

    if pair == 2:
        @pl.when(lax.rem(me, 2) == 0)
        def _():
            inner[...] = jnp.zeros_like(inner)

    place = lax.broadcasted_iota(jnp.int32, (SUB, LANES), 0)
    step = place.astype(jnp.float32)

    def ready(i):
        @pl.when(me > 0)
        def _():
            halo_copy(i).wait_recv()

    def state_copy(source, target):
        return pltpu.make_async_remote_copy(
            src_ref=sent.at[pl.ds(lax.rem(target, pair) * half, half)],
            dst_ref=arrived.at[source, pl.ds(lax.rem(target, pair) * half, half)],
            send_sem=state_send.at[target],
            recv_sem=state_recv.at[source],
            device_id=device(target),
            device_id_type=pl.DeviceIdType.MESH,
        )

    def pair_copy():
        return pltpu.make_async_remote_copy(
            src_ref=sent,
            dst_ref=inner,
            send_sem=pair_send.at[0],
            recv_sem=pair_recv.at[0],
            device_id=device(me + 1 - 2 * lax.rem(me, 2)),
            device_id_type=pl.DeviceIdType.MESH,
        )

    for i in (3, 5, 0, 1):
        fixed_loads[i].wait()

    backward = -step

    def filters(c, j):
        cols = columns(c)
        pace = rate[:, cols]
        twice = 2.0 * pace
        small = twice * (1.0 - twice * (0.5 - twice * (1.0 / 6.0 - twice * (1.0 / 24.0 - twice * (1.0 / 120.0)))))
        gap = jnp.where(twice < 0.03125, small, 1.0 - jnp.exp(-twice))
        rows_of = hold.at[j]
        rows_of[pl.ds(0, modes)] = residue[:, cols] * jnp.sqrt(gap)
        rows_of[pl.ds(modes, modes)] = jnp.exp(-pace)
        hops[c] = jnp.exp(-pace * float(SUB))
        total = jnp.zeros((SUB, LANES), jnp.float32)
        for m in range(modes):
            term = rows_of[pl.ds(m, 1)] * jnp.exp(rate[pl.ds(m, 1), cols] * backward)
            total = total + term
            terms[c, m] = term * rows_of[pl.ds(modes + m, 1)]
        rows_of[pl.ds(2 * modes, SUB)] = total
        for lag in range(SUB):
            tap = rows_of[pl.ds(2 * modes + lag, 1)]
            if lag == 0:
                tap = tap + skip[:, cols]
            near[c, pl.ds(lag, 1)] = tap

    twin = hold.shape[0]

    early = (lax.rem(me, chips) < pair) & (me >= pair)

    @pl.when(early)
    def _():
        @pl.loop(0, blocks // twin)
        def _(many):
            for j in range(twin):
                filters(many * twin + j, j)

    ready(4)
    ready(5)

    wide = 4 if blocks % 4 == 0 else 1

    def fixed_up(c, j):
        cols = columns(c)

        def opening(i, stream):
            at = 2 * j + i - 4
            ext[at, pl.ds(SUB, SUB)] = halo[i, :, cols].astype(jnp.float32)
            ext[at, pl.ds(2 * SUB, SUB)] = held[i, pl.ds(0, SUB), cols].astype(jnp.float32)
            total = li_feature[0, pl.ds(stream, 1), cols] * ext[at, pl.ds(2 * SUB, SUB)]
            for lag in (1, 2):
                total = total + li_feature[lag, pl.ds(stream, 1), cols] * ext[at, pl.ds(2 * SUB - lag, SUB)]
            return total

        right = (opening(4, 1) * opening(5, 2)).astype(jnp.bfloat16).astype(jnp.float32)
        extended[pl.ds(j * SUB, SUB)] = right - u_li[c, pl.ds(SUB, SUB)]
        u_li[c, pl.ds(SUB, SUB)] = right
        pace = rate[:, cols]
        moved = jnp.exp(-pace * float(SUB - 1)) * extended[pl.ds(j * SUB, 1)]
        moved = moved + jnp.exp(-pace * float(SUB - 2)) * extended[pl.ds(j * SUB + 1, 1)]
        shift[c] = moved
        state = own[c] + jnp.exp(-pace * float(rows - SUB)) * moved
        own[c] = state
        sent[c] = state.astype(sent.dtype)

    @pl.loop(0, blocks // wide)
    def _(many):
        for j in range(wide):
            fixed_up(many * wide + j, j)

    if pair == 2:
        @pl.when(lax.rem(me, 2) == 0)
        def _():
            pair_copy().start()

    @pl.when(jnp.logical_not(early))
    def _():
        @pl.loop(0, blocks // twin)
        def _(many):
            for j in range(twin):
                filters(many * twin + j, j)

    loads[3].wait()
    ready(3)

    def li_part(c):
        gates[c] = featurized(3, c, li_feature, 0, 0)
        taps = [near[c, pl.ds(lag, 1)] for lag in range(SUB)]
        for top in range(0, chunks, SUB):
            count = min(SUB, chunks - top)
            tokens = [u_li[c, pl.ds(SUB + top * SUB + b, count, SUB)] for b in range(SUB)]
            for b in range(SUB):
                total = taps[0] * tokens[b]
                for lag in range(1, b + 1):
                    total = total + taps[lag] * tokens[b - lag]
                partial[c, pl.ds(top * SUB + b, count, SUB)] = total

    middle = blocks // 2

    @pl.loop(0, middle)
    def _(c):
        li_part(c)

    if pair == 2:
        @pl.when(lax.rem(me, 2) == 1)
        def _():
            pair_copy().wait_recv()

            @pl.loop(0, blocks // wide)
            def _(many):
                for j in range(wide):
                    c = many * wide + j
                    fall = jnp.exp(-rate[:, columns(c)] * float(rows))
                    sent[c] = (fall * inner[c].astype(jnp.float32) + own[c]).astype(sent.dtype)

    leads = lax.rem(me, pair) == pair - 1
    slot = lax.div(me, pair)

    def send_states(first, last):
        @pl.when(leads)
        def _():
            @pl.loop(first, last)
            def _(target):
                state_copy(slot, target).start()

    if pair == 2:
        send_states(me + 1, jnp.where(me == 1, min(4, n), n))
    else:
        send_states(me + 1, n)

    @pl.loop(middle, blocks)
    def _(c):
        li_part(c)

    if pair == 2 and n > 4:
        @pl.when(me == 1)
        def _():
            pl.semaphore_wait(ready_sem, 1)
            send_states(4, n)

    step_by = 4 if half % 4 == 0 else 1

    def by_four(first, body):
        @pl.loop(0, half // step_by)
        def _(many):
            for j in range(step_by):
                body(first + many * step_by + j)

    def cleared(c):
        tally[c] = jnp.zeros((modes, LANES), jnp.float32)

    ours, theirs = side * half, (pair - 1 - side) * half
    by_four(ours, cleared)

    for i in (1, 2, 0):
        loads[i].wait()
        ready(i)

    @pl.loop(0, blocks)
    def _(c):
        cols = columns(c)
        product = featurized(1, c, se_feature, 1, SUB) * featurized(2, c, se_feature, 2, SUB)
        extended[...] = product.astype(jnp.bfloat16).astype(jnp.float32)
        mixed = se_filter[pl.ds(0, 1), cols] * extended[pl.ds(SUB, rows)]
        for lag in range(1, lags):
            mixed = mixed + se_filter[pl.ds(lag, 1), cols] * extended[pl.ds(SUB - lag, rows)]
        se[:, cols] = (featurized(0, c, se_feature, 0, 0) * mixed).astype(jnp.bfloat16)

    odd = lax.rem(jnp.full((modes, LANES), me, jnp.int32), 2) == 1
    def summed(source):
        def body(c):
            fall = jnp.exp(-rate[:, columns(c)] * float(rows * pair))
            total = fall * tally[c] + arrived[source, c].astype(jnp.float32)
            tally[c] = total
            lent[c] = total.astype(lent.dtype)

        return body

    def carried_in(c, before):
        if pair == 2:
            within = jnp.exp(-rate[:, columns(c)] * float(rows)) * before + inner[c].astype(jnp.float32)
            before = jnp.where(odd, within, before)
        carry[c] = before

    @pl.loop(0, slot)
    def _(source):
        state_copy(source, me).wait_recv()
        by_four(ours, summed(source))

    def swap_copy(first):
        return pltpu.make_async_remote_copy(
            src_ref=lent.at[pl.ds(first, half)],
            dst_ref=lent.at[pl.ds(first, half)],
            send_sem=swap_send.at[0],
            recv_sem=swap_recv.at[0],
            device_id=device(me + 1 - 2 * lax.rem(me, 2)),
            device_id_type=pl.DeviceIdType.MESH,
        )

    if pair == 2:
        @pl.when(slot > 0)
        def _():
            swap_copy(ours).start()

        @pl.when(slot == 0)
        def _():
            lent[...] = jnp.zeros_like(lent)

    by_four(ours, lambda c: carried_in(c, tally[c]))

    @pl.loop(0, half)
    def _(c):
        far(ours + c, partial, gates, terms, starts, shift, carry, hops, made, full)

    if pair == 2:
        @pl.when(slot > 0)
        def _():
            swap_copy(theirs).wait_recv()

        by_four(theirs, lambda c: carried_in(c, lent[c].astype(jnp.float32)))

        @pl.when(slot > 0)
        def _():
            swap_copy(ours).wait_send()

    @pl.when(me < n - 1)
    def _():
        for i in range(6):
            halo_copy(i).wait_send()

    if pair == 2:
        @pl.when(lax.rem(me, 2) == 0)
        def _():
            pair_copy().wait_send()

    @pl.when(leads)
    def _():
        @pl.loop(me + 1, n)
        def _(target):
            state_copy(slot, target).wait_send()


def finish(n, chips, se, made, partial, gates, terms, starts, shift, carry, hops, se_out, li_out, rest, full, sems):
    blocks = partial.shape[0]
    width = se.shape[1]
    pair = 2 if paired(n, blocks) else 1
    half = blocks // pair
    me = lax.axis_index("node") * chips + lax.axis_index("chip")
    ours = lax.rem(me, pair) * half
    theirs = half - ours

    def columns(first, count):
        return pl.ds(pl.multiple_of(first * LANES, LANES), count * LANES)

    own = columns(ours, half)
    done = [pltpu.make_async_copy(se, se_out, sems.at[0]), pltpu.make_async_copy(made.at[:, own], li_out.at[:, own], sems.at[1])]
    for copy in done:
        copy.start()
    if pair == 2:
        parts = sems.shape[0] - 2
        each = half // parts
        for part in range(parts):
            @pl.loop(part * each, (part + 1) * each)
            def _(c):
                far(theirs + c, partial, gates, terms, starts, shift, carry, hops, rest, full)

            cols = columns(theirs + part * each, each)
            done.append(pltpu.make_async_copy(rest.at[:, cols], li_out.at[:, cols], sems.at[2 + part]))
            done[-1].start()
    for copy in done:
        copy.wait()


def shards(*args):
    rows, width = args[0].shape
    modes = args[10].shape[0]
    n, chips = lax.axis_size(GROUP), lax.axis_size("chip")
    blocks, chunks = width // LANES, rows // SUB
    f32 = jnp.float32
    far = pl.BlockSpec(memory_space=pltpu.HBM)
    local = pl.BlockSpec(memory_space=pltpu.VMEM)
    operands = args[:11] + (args[11][None],)
    words = rows * width * 10 + width * modes * (3 * chunks + 3 * SUB + 8 + n)
    budget = min(4 * words + 8 * 2**20, 60 * 2**20)
    parts = 4 if blocks % 4 == 0 else 1
    passed = ((rows, width), jnp.bfloat16), ((rows, width), jnp.bfloat16), *(((blocks, *shape, LANES), f32) for shape in ((rows,), (rows,), (modes, SUB), (chunks, modes), (modes,), (modes,), (modes,)))
    mixed = pl.pallas_call(
        functools.partial(mixer, n, chips),
        out_shape=tuple(jax.ShapeDtypeStruct(*one) for one in passed),
        in_specs=[far] * 12,
        out_specs=(local,) * len(passed),
        scratch_shapes=[
            pltpu.VMEM((6, rows, width), jnp.bfloat16),
            pltpu.VMEM((6, SUB, width), jnp.bfloat16),
            pltpu.VMEM((n, blocks, modes, LANES), LINK),
            pltpu.VMEM((blocks, modes, LANES), LINK),
            pltpu.VMEM((8, rows + 2 * SUB, LANES), f32),
            pltpu.VMEM((rows + SUB, LANES), f32),
            pltpu.VMEM((blocks, rows + SUB, LANES), f32),
            pltpu.VMEM((blocks, SUB, LANES), f32),
            pltpu.VMEM((2 if blocks % 2 == 0 else 1, 2 * modes + SUB, LANES), f32),
            pltpu.VMEM((blocks, modes, LANES), f32),
            pltpu.VMEM((blocks, modes, LANES), LINK),
            pltpu.VMEM((blocks, modes, LANES), f32),
            pltpu.VMEM((blocks, modes, LANES), LINK),
            pltpu.VMEM((chunks, modes, LANES), f32),
            *[pltpu.VMEM(array.shape, f32) for array in operands[6:]],
            pltpu.SemaphoreType.DMA((4,)),
            pltpu.SemaphoreType.DMA((2, parts)),
            pltpu.SemaphoreType.DMA((6,)),
            pltpu.SemaphoreType.DMA((6,)),
            pltpu.SemaphoreType.DMA((6,)),
            pltpu.SemaphoreType.DMA((1,)),
            pltpu.SemaphoreType.DMA((1,)),
            pltpu.SemaphoreType.DMA((n,)),
            pltpu.SemaphoreType.DMA((n,)),
            pltpu.SemaphoreType.DMA((1,)),
            pltpu.SemaphoreType.DMA((1,)),
            pltpu.SemaphoreType.REGULAR,
        ],
        compiler_params=pltpu.CompilerParams(collective_id=0, has_side_effects=True, vmem_limit_bytes=budget),
        name="mixer",
    )(*(pltpu.with_memory_space_constraint(array, pltpu.HBM) for array in operands))
    return pl.pallas_call(
        functools.partial(finish, n, chips),
        out_shape=(jax.ShapeDtypeStruct((rows, width), jnp.bfloat16),) * 2,
        in_specs=[local] * len(passed),
        out_specs=(far, far),
        scratch_shapes=[
            pltpu.VMEM((rows, width), jnp.bfloat16),
            pltpu.VMEM((chunks, modes, LANES), f32),
            pltpu.SemaphoreType.DMA((2 + (2 if blocks % 4 == 0 else 1),)),
        ],
        compiler_params=pltpu.CompilerParams(vmem_limit_bytes=8 * 2**20),
        name="finish",
    )(*mixed)


def solution(mesh):
    placed = (P(("dp", "node", "chip"), None),) * 6 + (P(),) * 6
    return jax.shard_map(
        shards,
        mesh=mesh,
        in_specs=placed,
        out_specs=(P(("dp", "node", "chip"), None), P(("dp", "node", "chip"), None)),
        check_vma=False,
    )
```

```python
import functools

import jax
import jax.numpy as jnp
from jax import lax
from jax.experimental import pallas as pl
from jax.experimental.pallas import tpu as pltpu
from jax.sharding import PartitionSpec as P

LANES = 128
SUB = 8
LINK = jnp.bfloat16
GROUP = ("node", "chip")


def paired(n, blocks):
    return n % 2 == 0 and blocks % 2 == 0


def far(c, partial, gates, terms, starts, shift, carry, hops, made, full):
    chunks, modes = starts.shape[1], starts.shape[2]
    earlier = carry[c]
    hop = hops[c]
    for a in range(chunks):
        full[a] = starts[c, a] + earlier
        earlier = hop * earlier
        if a == 0:
            earlier = earlier + shift[c]
    cols = pl.ds(pl.multiple_of(c * LANES, LANES), LANES)
    for top in range(0, chunks, SUB):
        span = range(top, min(top + SUB, chunks))
        totals = [partial[c, pl.ds(a * SUB, SUB)] for a in span]
        for m in range(modes):
            term = terms[c, m]
            totals = [total + term * full[a, pl.ds(m, 1)] for a, total in zip(span, totals)]
        first = pl.ds(top * SUB, len(span) * SUB)
        made[first, cols] = (gates[c, first] * jnp.concatenate(totals)).astype(jnp.bfloat16)


def mixer(n, chips, *refs):
    streams, kept = refs[:6], refs[6:12]
    se, made, partial, gates, terms, starts, shift, carry, hops = refs[12:21]
    (
        held, halo, arrived, sent, ext, extended, u_li, near, hold, own, inner, tally, lent, full,
        se_feature, se_filter, li_feature, residue, rate, skip, in_sem, part_sem, fixed_sem, halo_send, halo_recv, pair_send, pair_recv, state_send, state_recv, swap_send, swap_recv, ready_sem,
    ) = refs[21:]
    rows, width = held.shape[1], held.shape[2]
    blocks = width // LANES
    chunks = rows // SUB
    modes = rate.shape[0]
    lags = se_filter.shape[0]
    pair = 2 if paired(n, blocks) else 1
    half = blocks // pair
    dp = lax.axis_index("dp")
    me = lax.axis_index("node") * chips + lax.axis_index("chip")

    def device(index):
        return (dp, lax.div(index, chips), lax.rem(index, chips))

    order = (4, 5, 3, 1, 2, 0)
    parts = part_sem.shape[1]
    each = width // parts
    loads = [pltpu.make_async_copy(streams[i], held.at[i], in_sem.at[i]) for i in range(4)]

    def piece(i, part):
        cols = pl.ds(part * each, each)
        return pltpu.make_async_copy(streams[i].at[:, cols], held.at[i, :, cols], part_sem.at[i - 4, part])

    fixed = (se_feature, se_filter, li_feature, residue, rate, skip)
    fixed_loads = [pltpu.make_async_copy(kept[i], fixed[i], fixed_sem.at[i]) for i in range(6)]
    for i in (4, 2):
        fixed_loads[i].start()
    for part in range(parts):
        for i in (4, 5):
            piece(i, part).start()

    barrier = pltpu.get_barrier_semaphore()

    side = lax.rem(me, pair)
    odd_core = lax.rem(me, 2) == 1

    def hail(semaphore, other):
        pl.semaphore_signal(semaphore, inc=1, device_id=device(other), device_id_type=pl.DeviceIdType.MESH)

    def hail_if(condition, semaphore, other):
        @pl.when(condition)
        def _():
            hail(semaphore, other)

    if pair == 2:
        hail_if(me > 0, barrier, me - 1)
        hail_if(jnp.logical_not(odd_core), barrier, me + 1)
        hail_if(odd_core & (me > 1), barrier, me - 2)
        hail_if(odd_core & (me < n - 1), barrier, me + 2)
    else:
        @pl.loop(0, n)
        def _(other):
            hail_if(other != me, barrier, other)

    def meet():
        if pair == 2:
            pl.semaphore_wait(barrier, jnp.where(odd_core, 1 + 2 * (me < n - 1).astype(jnp.int32) + (me > 1).astype(jnp.int32), 1))
            if n > 4:
                hail_if(me == n - 3, ready_sem, me - 2)
        else:
            pl.semaphore_wait(barrier, n - 1)

    for i in range(6):
        ext[i, pl.ds(0, 2 * SUB)] = jnp.zeros((2 * SUB, LANES), jnp.float32)

    def columns(c):
        return pl.ds(pl.multiple_of(c * LANES, LANES), LANES)

    def featurized(i, c, taps, stream, early):
        cols = columns(c)
        if i not in (4, 5):
            ext[i, pl.ds(SUB, SUB)] = halo[i, :, cols].astype(jnp.float32)
        ext[i, pl.ds(2 * SUB, rows)] = held[i, :, cols].astype(jnp.float32)
        first, count = 2 * SUB - early, rows + early
        total = taps[0, pl.ds(stream, 1), cols] * ext[i, pl.ds(first, count)]
        for lag in (1, 2):
            total = total + taps[lag, pl.ds(stream, 1), cols] * ext[i, pl.ds(first - lag, count)]
        return total

    def local_states(c):
        cols = columns(c)
        product = featurized(4, c, li_feature, 1, 0) * featurized(5, c, li_feature, 2, 0)
        u_li[c, pl.ds(0, SUB)] = jnp.zeros((SUB, LANES), jnp.float32)
        u_li[c, pl.ds(SUB, rows)] = product.astype(jnp.bfloat16).astype(jnp.float32)
        pace = rate[:, cols]
        powers = [None] + [jnp.exp(-pace * float(k)) for k in range(1, SUB + 1)]
        state = jnp.zeros((modes, LANES), jnp.float32)
        for a in range(chunks):
            starts[c, a] = state
            new = jnp.broadcast_to(u_li[c, pl.ds(SUB + a * SUB + SUB - 1, 1)], (modes, LANES))
            for b in range(SUB - 1):
                new = new + powers[SUB - 1 - b] * u_li[c, pl.ds(SUB + a * SUB + b, 1)]
            state = powers[SUB] * state + new
        own[c] = state

    tail = (2, SUB, SUB, 2, 2, 2)

    def halo_copy(i):
        return pltpu.make_async_remote_copy(
            src_ref=streams[i].at[pl.ds(rows - tail[i], tail[i])],
            dst_ref=halo.at[i, pl.ds(SUB - tail[i], tail[i])],
            send_sem=halo_send.at[i],
            recv_sem=halo_recv.at[i],
            device_id=device(lax.rem(me + 1, n)),
            device_id_type=pl.DeviceIdType.MESH,
        )

    per = blocks // parts

    def states(first, last):
        @pl.loop(first, last)
        def _(c):
            local_states(c)

    for i in (4, 2):
        fixed_loads[i].wait()
    for part in range(parts):
        for i in (4, 5):
            piece(i, part).wait()
        if part == 0:
            for i in (3, 5, 0, 1):
                fixed_loads[i].start()
            for i in (3, 1, 2, 0):
                loads[i].start()
            states(0, per)
            meet()

            @pl.when(me < n - 1)
            def _():
                for i in order:
                    halo_copy(i).start()
        else:
            states(part * per, (part + 1) * per)

    if pair == 2:
        @pl.when(odd_core & (me > 1) & (me < n - 4))
        def _():
            pl.semaphore_wait(ready_sem, 1)
            hail(ready_sem, me - 2)

    @pl.when(me == 0)
    def _():
        halo[...] = jnp.zeros_like(halo)

    if pair == 2:
        @pl.when(lax.rem(me, 2) == 0)
        def _():
            inner[...] = jnp.zeros_like(inner)

    place = lax.broadcasted_iota(jnp.int32, (SUB, LANES), 0)
    step = place.astype(jnp.float32)

    def ready(i):
        @pl.when(me > 0)
        def _():
            halo_copy(i).wait_recv()

    def state_copy(source, target):
        return pltpu.make_async_remote_copy(
            src_ref=sent.at[pl.ds(lax.rem(target, pair) * half, half)],
            dst_ref=arrived.at[source, pl.ds(lax.rem(target, pair) * half, half)],
            send_sem=state_send.at[target],
            recv_sem=state_recv.at[source],
            device_id=device(target),
            device_id_type=pl.DeviceIdType.MESH,
        )

    def pair_copy():
        return pltpu.make_async_remote_copy(
            src_ref=sent,
            dst_ref=inner,
            send_sem=pair_send.at[0],
            recv_sem=pair_recv.at[0],
            device_id=device(me + 1 - 2 * lax.rem(me, 2)),
            device_id_type=pl.DeviceIdType.MESH,
        )

    for i in (3, 5, 0, 1):
        fixed_loads[i].wait()

    backward = -step

    def filters(c, j):
        cols = columns(c)
        pace = rate[:, cols]
        twice = 2.0 * pace
        small = twice * (1.0 - twice * (0.5 - twice * (1.0 / 6.0 - twice * (1.0 / 24.0 - twice * (1.0 / 120.0)))))
        gap = jnp.where(twice < 0.03125, small, 1.0 - jnp.exp(-twice))
        rows_of = hold.at[j]
        rows_of[pl.ds(0, modes)] = residue[:, cols] * jnp.sqrt(gap)
        rows_of[pl.ds(modes, modes)] = jnp.exp(-pace)
        hops[c] = jnp.exp(-pace * float(SUB))
        total = jnp.zeros((SUB, LANES), jnp.float32)
        for m in range(modes):
            term = rows_of[pl.ds(m, 1)] * jnp.exp(rate[pl.ds(m, 1), cols] * backward)
            total = total + term
            terms[c, m] = term * rows_of[pl.ds(modes + m, 1)]
        rows_of[pl.ds(2 * modes, SUB)] = total
        for lag in range(SUB):
            tap = rows_of[pl.ds(2 * modes + lag, 1)]
            if lag == 0:
                tap = tap + skip[:, cols]
            near[c, pl.ds(lag, 1)] = tap

    twin = hold.shape[0]

    early = (lax.rem(me, chips) < pair) & (me >= pair)

    @pl.when(early)
    def _():
        @pl.loop(0, blocks // twin)
        def _(many):
            for j in range(twin):
                filters(many * twin + j, j)

    ready(4)
    ready(5)

    wide = 4 if blocks % 4 == 0 else 1

    def fixed_up(c, j):
        cols = columns(c)

        def opening(i, stream):
            at = 2 * j + i - 4
            ext[at, pl.ds(SUB, SUB)] = halo[i, :, cols].astype(jnp.float32)
            ext[at, pl.ds(2 * SUB, SUB)] = held[i, pl.ds(0, SUB), cols].astype(jnp.float32)
            total = li_feature[0, pl.ds(stream, 1), cols] * ext[at, pl.ds(2 * SUB, SUB)]
            for lag in (1, 2):
                total = total + li_feature[lag, pl.ds(stream, 1), cols] * ext[at, pl.ds(2 * SUB - lag, SUB)]
            return total

        right = (opening(4, 1) * opening(5, 2)).astype(jnp.bfloat16).astype(jnp.float32)
        extended[pl.ds(j * SUB, SUB)] = right - u_li[c, pl.ds(SUB, SUB)]
        u_li[c, pl.ds(SUB, SUB)] = right
        pace = rate[:, cols]
        moved = jnp.exp(-pace * float(SUB - 1)) * extended[pl.ds(j * SUB, 1)]
        moved = moved + jnp.exp(-pace * float(SUB - 2)) * extended[pl.ds(j * SUB + 1, 1)]
        shift[c] = moved
        state = own[c] + jnp.exp(-pace * float(rows - SUB)) * moved
        own[c] = state
        sent[c] = state.astype(sent.dtype)

    @pl.loop(0, blocks // wide)
    def _(many):
        for j in range(wide):
            fixed_up(many * wide + j, j)

    if pair == 2:
        @pl.when(lax.rem(me, 2) == 0)
        def _():
            pair_copy().start()

    @pl.when(jnp.logical_not(early))
    def _():
        @pl.loop(0, blocks // twin)
        def _(many):
            for j in range(twin):
                filters(many * twin + j, j)

    loads[3].wait()
    ready(3)

    def li_part(c):
        gates[c] = featurized(3, c, li_feature, 0, 0)
        taps = [near[c, pl.ds(lag, 1)] for lag in range(SUB)]
        for top in range(0, chunks, SUB):
            count = min(SUB, chunks - top)
            tokens = [u_li[c, pl.ds(SUB + top * SUB + b, count, SUB)] for b in range(SUB)]
            for b in range(SUB):
                total = taps[0] * tokens[b]
                for lag in range(1, b + 1):
                    total = total + taps[lag] * tokens[b - lag]
                partial[c, pl.ds(top * SUB + b, count, SUB)] = total

    middle = 3 * blocks // 4

    @pl.loop(0, middle)
    def _(c):
        li_part(c)

    if pair == 2:
        @pl.when(lax.rem(me, 2) == 1)
        def _():
            pair_copy().wait_recv()

            @pl.loop(0, blocks // wide)
            def _(many):
                for j in range(wide):
                    c = many * wide + j
                    fall = jnp.exp(-rate[:, columns(c)] * float(rows))
                    sent[c] = (fall * inner[c].astype(jnp.float32) + own[c]).astype(sent.dtype)

    leads = lax.rem(me, pair) == pair - 1
    slot = lax.div(me, pair)

    def send_states(first, last):
        @pl.when(leads)
        def _():
            @pl.loop(first, last)
            def _(target):
                state_copy(slot, target).start()

    if pair == 2:
        send_states(me + 1, jnp.where(me == 1, min(4, n), n))
    else:
        send_states(me + 1, n)

    @pl.loop(middle, blocks)
    def _(c):
        li_part(c)

    if pair == 2 and n > 4:
        @pl.when(me == 1)
        def _():
            pl.semaphore_wait(ready_sem, 1)
            send_states(4, n)

    step_by = 4 if half % 4 == 0 else 1

    def by_four(first, body):
        @pl.loop(0, half // step_by)
        def _(many):
            for j in range(step_by):
                body(first + many * step_by + j)

    def cleared(c):
        tally[c] = jnp.zeros((modes, LANES), jnp.float32)

    ours, theirs = side * half, (pair - 1 - side) * half
    by_four(ours, cleared)

    for i in (1, 2, 0):
        loads[i].wait()
        ready(i)

    @pl.loop(0, blocks)
    def _(c):
        cols = columns(c)
        product = featurized(1, c, se_feature, 1, SUB) * featurized(2, c, se_feature, 2, SUB)
        extended[...] = product.astype(jnp.bfloat16).astype(jnp.float32)
        mixed = se_filter[pl.ds(0, 1), cols] * extended[pl.ds(SUB, rows)]
        for lag in range(1, lags):
            mixed = mixed + se_filter[pl.ds(lag, 1), cols] * extended[pl.ds(SUB - lag, rows)]
        se[:, cols] = (featurized(0, c, se_feature, 0, 0) * mixed).astype(jnp.bfloat16)

    odd = lax.rem(jnp.full((modes, LANES), me, jnp.int32), 2) == 1
    def summed(source):
        def body(c):
            fall = jnp.exp(-rate[:, columns(c)] * float(rows * pair))
            total = fall * tally[c] + arrived[source, c].astype(jnp.float32)
            tally[c] = total
            lent[c] = total.astype(lent.dtype)

        return body

    def carried_in(c, before):
        if pair == 2:
            within = jnp.exp(-rate[:, columns(c)] * float(rows)) * before + inner[c].astype(jnp.float32)
            before = jnp.where(odd, within, before)
        carry[c] = before

    @pl.loop(0, slot)
    def _(source):
        state_copy(source, me).wait_recv()
        by_four(ours, summed(source))

    def swap_copy(first):
        return pltpu.make_async_remote_copy(
            src_ref=lent.at[pl.ds(first, half)],
            dst_ref=lent.at[pl.ds(first, half)],
            send_sem=swap_send.at[0],
            recv_sem=swap_recv.at[0],
            device_id=device(me + 1 - 2 * lax.rem(me, 2)),
            device_id_type=pl.DeviceIdType.MESH,
        )

    if pair == 2:
        @pl.when(slot > 0)
        def _():
            swap_copy(ours).start()

        @pl.when(slot == 0)
        def _():
            lent[...] = jnp.zeros_like(lent)

    by_four(ours, lambda c: carried_in(c, tally[c]))

    @pl.loop(0, half)
    def _(c):
        far(ours + c, partial, gates, terms, starts, shift, carry, hops, made, full)

    if pair == 2:
        @pl.when(slot > 0)
        def _():
            swap_copy(theirs).wait_recv()

        by_four(theirs, lambda c: carried_in(c, lent[c].astype(jnp.float32)))

        @pl.when(slot > 0)
        def _():
            swap_copy(ours).wait_send()

    @pl.when(me < n - 1)
    def _():
        for i in range(6):
            halo_copy(i).wait_send()

    if pair == 2:
        @pl.when(lax.rem(me, 2) == 0)
        def _():
            pair_copy().wait_send()

    @pl.when(leads)
    def _():
        @pl.loop(me + 1, n)
        def _(target):
            state_copy(slot, target).wait_send()


def finish(n, chips, se, made, partial, gates, terms, starts, shift, carry, hops, se_out, li_out, rest, full, sems):
    blocks = partial.shape[0]
    width = se.shape[1]
    pair = 2 if paired(n, blocks) else 1
    half = blocks // pair
    me = lax.axis_index("node") * chips + lax.axis_index("chip")
    ours = lax.rem(me, pair) * half
    theirs = half - ours

    def columns(first, count):
        return pl.ds(pl.multiple_of(first * LANES, LANES), count * LANES)

    own = columns(ours, half)
    done = [pltpu.make_async_copy(se, se_out, sems.at[0]), pltpu.make_async_copy(made.at[:, own], li_out.at[:, own], sems.at[1])]
    for copy in done:
        copy.start()
    if pair == 2:
        parts = sems.shape[0] - 2
        each = half // parts
        for part in range(parts):
            @pl.loop(part * each, (part + 1) * each)
            def _(c):
                far(theirs + c, partial, gates, terms, starts, shift, carry, hops, rest, full)

            cols = columns(theirs + part * each, each)
            done.append(pltpu.make_async_copy(rest.at[:, cols], li_out.at[:, cols], sems.at[2 + part]))
            done[-1].start()
    for copy in done:
        copy.wait()


def shards(*args):
    rows, width = args[0].shape
    modes = args[10].shape[0]
    n, chips = lax.axis_size(GROUP), lax.axis_size("chip")
    blocks, chunks = width // LANES, rows // SUB
    f32 = jnp.float32
    far = pl.BlockSpec(memory_space=pltpu.HBM)
    local = pl.BlockSpec(memory_space=pltpu.VMEM)
    operands = args[:11] + (args[11][None],)
    words = rows * width * 10 + width * modes * (3 * chunks + 3 * SUB + 8 + n)
    budget = min(4 * words + 8 * 2**20, 60 * 2**20)
    parts = 4 if blocks % 4 == 0 else 1
    passed = ((rows, width), jnp.bfloat16), ((rows, width), jnp.bfloat16), *(((blocks, *shape, LANES), f32) for shape in ((rows,), (rows,), (modes, SUB), (chunks, modes), (modes,), (modes,), (modes,)))
    mixed = pl.pallas_call(
        functools.partial(mixer, n, chips),
        out_shape=tuple(jax.ShapeDtypeStruct(*one) for one in passed),
        in_specs=[far] * 12,
        out_specs=(local,) * len(passed),
        scratch_shapes=[
            pltpu.VMEM((6, rows, width), jnp.bfloat16),
            pltpu.VMEM((6, SUB, width), jnp.bfloat16),
            pltpu.VMEM((n, blocks, modes, LANES), LINK),
            pltpu.VMEM((blocks, modes, LANES), LINK),
            pltpu.VMEM((8, rows + 2 * SUB, LANES), f32),
            pltpu.VMEM((rows + SUB, LANES), f32),
            pltpu.VMEM((blocks, rows + SUB, LANES), f32),
            pltpu.VMEM((blocks, SUB, LANES), f32),
            pltpu.VMEM((2 if blocks % 2 == 0 else 1, 2 * modes + SUB, LANES), f32),
            pltpu.VMEM((blocks, modes, LANES), f32),
            pltpu.VMEM((blocks, modes, LANES), LINK),
            pltpu.VMEM((blocks, modes, LANES), f32),
            pltpu.VMEM((blocks, modes, LANES), LINK),
            pltpu.VMEM((chunks, modes, LANES), f32),
            *[pltpu.VMEM(array.shape, f32) for array in operands[6:]],
            pltpu.SemaphoreType.DMA((4,)),
            pltpu.SemaphoreType.DMA((2, parts)),
            pltpu.SemaphoreType.DMA((6,)),
            pltpu.SemaphoreType.DMA((6,)),
            pltpu.SemaphoreType.DMA((6,)),
            pltpu.SemaphoreType.DMA((1,)),
            pltpu.SemaphoreType.DMA((1,)),
            pltpu.SemaphoreType.DMA((n,)),
            pltpu.SemaphoreType.DMA((n,)),
            pltpu.SemaphoreType.DMA((1,)),
            pltpu.SemaphoreType.DMA((1,)),
            pltpu.SemaphoreType.REGULAR,
        ],
        compiler_params=pltpu.CompilerParams(collective_id=0, has_side_effects=True, vmem_limit_bytes=budget),
        name="mixer",
    )(*(pltpu.with_memory_space_constraint(array, pltpu.HBM) for array in operands))
    return pl.pallas_call(
        functools.partial(finish, n, chips),
        out_shape=(jax.ShapeDtypeStruct((rows, width), jnp.bfloat16),) * 2,
        in_specs=[local] * len(passed),
        out_specs=(far, far),
        scratch_shapes=[
            pltpu.VMEM((rows, width), jnp.bfloat16),
            pltpu.VMEM((chunks, modes, LANES), f32),
            pltpu.SemaphoreType.DMA((2 + (2 if blocks % 4 == 0 else 1),)),
        ],
        compiler_params=pltpu.CompilerParams(vmem_limit_bytes=8 * 2**20),
        name="finish",
    )(*mixed)


def solution(mesh):
    placed = (P(("dp", "node", "chip"), None),) * 6 + (P(),) * 6
    return jax.shard_map(
        shards,
        mesh=mesh,
        in_specs=placed,
        out_specs=(P(("dp", "node", "chip"), None), P(("dp", "node", "chip"), None)),
        check_vma=False,
    )
```
